256 devices in a mesh: cells: 32 (over z, y), mem: 8 (over x, core).
Axes of the slice: x: 4, y: 4, z: 8, core: 2. Of those that a mesh axis runs over, the one named last changes fastest.
Arguments:
- background_copies: bfloat16 [512, 262144], P('mem', 'cells')
- measuring_span_leading_cell: int32 [131072], P(('cells', 'mem')), may hold values from 0 to 1023, as said below
- measuring_kernel_coefficients: bfloat16 [131072, 4], P(('cells', 'mem')), may hold values from -3 to 3
- measured_readings: float32 [131072], P(('cells', 'mem')), may hold values from -18 to 18
- measured_error_precision: float32 [131072], P(('cells', 'mem')), may hold values from 0.00078125 to 0.0078125
Outputs:
- analysis: float32 [512, 262144], P(None, ('cells', 'mem'))
The draws below stay inside these ranges and needn't reach their ends.
Inputs may be any that keep to these rules, and one draw needn't show every extreme that they name: `measuring_span_leading_cell`: in every block of 512 observations the first one's window starts at one of the last 3 cells of the block and the second one's at the block's last cell.
All inputs are finite; a program needn't handle non-finite values.
Results may differ from the reference program's by a relative error of at most 0.0014.
The reference program's roundings to bfloat16 on the way count: a program that leaves them out, or rounds other values in their place, can miss the bound.
Values may be sent and summed in bfloat16 or wider, within the bound.
A program may use at most 64 MiB of HBM per device.

```python
import math
import jax
import jax.numpy as jnp
from jax import lax

M = 512
STENCIL_LENGTH = 4
CD = 1024
NOBS_DEV = 512
NCELL = 262144
NOBS = 131072
N_CELLS = 32
N_MEM = 8


def draw_background_copies(key, part):
    key_scale, key_cell, key_noise, key_mode, key_shape, key_base, key_choose, key_load, key_pattern = jax.random.split(key, 9)
    member_scale = jnp.exp(jax.random.uniform(key_scale, (M, 1), jnp.float32, math.log(0.3), math.log(3.0)))
    noise = jax.random.normal(key_noise, (M, NCELL), jnp.float32)
    mode_weight = 0.8
    spectrum_top = 2.0
    cell_scale = jnp.exp(jax.random.uniform(key_cell, (1, NCELL), jnp.float32, math.log(0.5), math.log(2.0)))
    member_mode = jax.random.normal(key_mode, (M, 1), jnp.float32)
    cell_mode = jax.random.normal(key_shape, (1, NCELL), jnp.float32)
    base_state = 2.0 * jax.random.normal(key_base, (1, NCELL), jnp.float32)
    mode_choice = jax.random.randint(key_choose, (NCELL,), 0, M, dtype=jnp.int32)
    amplitude = spectrum_top / jnp.sqrt(1.0 + jnp.arange(M, dtype=jnp.float32) / 64.0)
    loadings = jax.random.normal(key_load, (M, M), jnp.float32) * amplitude[None, :]
    pattern = jax.random.normal(key_pattern, (1, NCELL), jnp.float32)
    many_modes = jnp.take(loadings, mode_choice, axis=1) * pattern
    return (base_state + member_scale * cell_scale * noise + many_modes + mode_weight * member_mode * cell_mode).astype(jnp.bfloat16)


def draw_measuring_span_leading_cell(key, part):
    key_free, key_near = jax.random.split(key)
    anywhere = jax.random.randint(key_free, (NOBS,), 0, CD, dtype=jnp.int32)
    near_end = CD - 1 - jax.random.randint(key_near, (NOBS,), 0, STENCIL_LENGTH - 1, dtype=jnp.int32)
    within = jnp.arange(NOBS, dtype=jnp.int32) % NOBS_DEV
    return jnp.where(within == 0, near_end, jnp.where(within == 1, CD - 1, anywhere))


def block_levels(rng, shape, cuts, least, top_value):
    gain, own = 1.0, jax.random.fold_in(rng, 6)
    for dim, parts in cuts:
        heights = jnp.exp(jax.random.uniform(jax.random.fold_in(own, dim), (parts,), jnp.float32, least / len(cuts), top_value / len(cuts)))
        gain = gain * jnp.repeat(heights, shape[dim] // parts).reshape([-1 if axis == dim else 1 for axis in range(len(shape))])
    return gain


def centred(rng, dims, scale, limit, cuts=(), kind=jnp.bfloat16):
    result = scale * jax.random.normal(rng, dims, jnp.float32)
    if cuts:
        result = result * block_levels(rng, dims, cuts, -0.22, 0.18)
    return jnp.clip(result, -limit, limit).astype(kind)


def setup_inputs(seed: int = 0) -> dict:
    keys = jax.random.split(jax.random.key(seed), 6)
    background_copies = draw_background_copies(jax.random.fold_in(keys[5], 71), 0)
    measuring_span_leading_cell = draw_measuring_span_leading_cell(jax.random.fold_in(keys[5], 71), 0)
    measuring_kernel_coefficients = centred(keys[2], (NOBS, STENCIL_LENGTH), STENCIL_LENGTH ** -0.5, 3.0, ((0, 256),))
    measured_readings = centred(keys[3], (NOBS,), 3.0, 18.0, ((0, 256),), jnp.float32)
    measured_error_precision = jnp.clip(jnp.exp(math.log(0.0078125) - 2.3025851 * jax.random.uniform(keys[4], (NOBS,), jnp.float32) ** block_levels(keys[4], (NOBS,), ((0, 256),), -0.2, 0.2)), 0.00078125, 0.0078125)
    return {"background_copies": background_copies, "measuring_span_leading_cell": measuring_span_leading_cell, "measuring_kernel_coefficients": measuring_kernel_coefficients, "measured_readings": measured_readings, "measured_error_precision": measured_error_precision}


def backsubstitute_lower(matrix, right, bottom_triangle):
    return lax.linalg.triangular_solve(matrix, right, left_side=True, lower=bottom_triangle)

def operator_table(offsets, weights, first_column, columns):
    position = lax.broadcasted_iota(jnp.int32, (offsets.shape[0], columns), 1) + first_column
    table = jnp.zeros((offsets.shape[0], columns), jnp.bfloat16)
    for window_step in range(weights.shape[1]):
        table = table + jnp.where(position == offsets[:, None] + window_step, weights[:, window_step:window_step + 1], jnp.zeros((), jnp.bfloat16))
    return table

def reference(background_copies, measuring_span_leading_cell, measuring_kernel_coefficients, measured_readings, measured_error_precision):
    predicted_copies = background_copies.shape[0]
    blocks = N_CELLS * N_MEM
    predicted_centroid = lax.optimization_barrier(jnp.sum(background_copies.astype(jnp.float32), axis=0)) / predicted_copies
    copy_anomalies = (background_copies.astype(jnp.float32) - predicted_centroid[None, :]).astype(jnp.bfloat16)
    anomaly_ext = jnp.concatenate([copy_anomalies, copy_anomalies[:, :STENCIL_LENGTH - 1]], axis=1)
    centroid_extended = jnp.concatenate([predicted_centroid, predicted_centroid[:STENCIL_LENGTH - 1]], axis=0)

    def block_terms(carry, block_index):
        gram_acc, pull_acc = carry
        start = (block_index * CD).astype(jnp.int32)
        obs_start = (block_index * NOBS_DEV).astype(jnp.int32)
        anomaly_block = lax.dynamic_slice_in_dim(anomaly_ext, start, CD + STENCIL_LENGTH - 1, 1)
        mean_block = lax.dynamic_slice_in_dim(centroid_extended, start, CD + STENCIL_LENGTH - 1, 0)
        offsets = lax.dynamic_slice_in_dim(measuring_span_leading_cell, obs_start, NOBS_DEV, 0)
        weights = lax.dynamic_slice_in_dim(measuring_kernel_coefficients, obs_start, NOBS_DEV, 0)
        values = lax.dynamic_slice_in_dim(measured_readings, obs_start, NOBS_DEV, 0)
        rinv = lax.dynamic_slice_in_dim(measured_error_precision, obs_start, NOBS_DEV, 0)
        table = operator_table(offsets, weights, 0, CD + STENCIL_LENGTH - 1)
        projected = jnp.dot(table.astype(jnp.float32), anomaly_block.T.astype(jnp.float32), preferred_element_type=jnp.float32)
        observed_mean = jnp.dot(table.astype(jnp.float32), mean_block, precision=lax.Precision.HIGHEST)
        root = jnp.sqrt(rinv)
        weighted = (root[:, None] * projected).astype(jnp.bfloat16)
        innovation = (root * (values - observed_mean)).astype(jnp.bfloat16)
        gram_acc = gram_acc + jnp.dot(weighted.T.astype(jnp.float32), weighted.astype(jnp.float32), preferred_element_type=jnp.float32)
        pull_acc = pull_acc + jnp.dot(innovation.astype(jnp.float32), weighted.astype(jnp.float32), preferred_element_type=jnp.float32)
        return ((gram_acc, pull_acc), None)
    initial_accumulator = (jnp.zeros((predicted_copies, predicted_copies), jnp.float32), jnp.zeros((predicted_copies,), jnp.float32))
    (inner_product_matrix, pull), _ = lax.scan(block_terms, initial_accumulator, jnp.arange(blocks, dtype=jnp.int32))
    linear_equations = inner_product_matrix + (predicted_copies - 1.0) * jnp.eye(predicted_copies, dtype=jnp.float32)
    triangle_matrix = jnp.linalg.cholesky(linear_equations)
    middle = backsubstitute_lower(triangle_matrix, pull[:, None], bottom_triangle=True)
    stencil_displacement = backsubstitute_lower(triangle_matrix.T, middle, bottom_triangle=False)[:, 0]
    reciprocal_matrix = backsubstitute_lower(triangle_matrix.T, jnp.eye(predicted_copies, dtype=jnp.float32), bottom_triangle=False)
    blend_matrix = (math.sqrt(predicted_copies - 1.0) * reciprocal_matrix + stencil_displacement[:, None]).astype(jnp.bfloat16)
    return predicted_centroid[None, :] + jnp.dot(blend_matrix.T.astype(jnp.float32), copy_anomalies.astype(jnp.float32), preferred_element_type=jnp.float32)
```

```python
import functools
import math

import jax
import jax.numpy as jnp
from jax import lax
from jax.experimental import pallas as pl
from jax.experimental.pallas import tpu as pltpu
from jax.sharding import PartitionSpec as P

F32 = jnp.float32
N_Y = 4
ROWS, LANES = 8, 128
MESH = pl.DeviceIdType.MESH


def passed_along(value, axis, steps):
    count = lax.axis_size(axis)
    pairs = [(source, (source + steps) % count) for source in range(count)]
    return lax.ppermute(value, axis, pairs)


def operator_table(offsets, weights, first_column, columns):
    position = lax.broadcasted_iota(jnp.int32, (offsets.shape[0], columns), 1) + first_column
    table = jnp.zeros((offsets.shape[0], columns), jnp.bfloat16)
    for window_step in range(weights.shape[1]):
        table = table + jnp.where(
            position == offsets[:, None] + window_step,
            weights[:, window_step : window_step + 1],
            jnp.zeros((), jnp.bfloat16),
        )
    return table


def total_kernel(n, n_mem, n_y, n_z, gram_ref, pull_ref, total_ref, pulled_ref,
                 share, mem_in, y_out, y_in, z_in,
                 mem_send, mem_recv, y_send, y_recv, z_send, z_recv, yg_send, yg_recv, mg_send, mg_recv):
    cell, mem = lax.axis_index("cells"), lax.axis_index("mem")
    y, z = lax.rem(cell, n_y), cell // n_y
    piece = share.shape[1] - ROWS
    part = piece // n_y

    def mem_peer(step):
        return (cell, lax.rem(mem + step, n_mem))

    def y_peer(step):
        return (z * n_y + lax.rem(y + step, n_y), mem)

    def z_peer(step):
        return (lax.rem(z + step, n_z) * n_y + y, mem)

    peers = (
        [mem_peer(s) for s in range(1, n_mem)]
        + [y_peer(s) for s in range(1, n_y)]
        + [z_peer(s) for s in range(1, n_z)]
    )
    barrier = pltpu.get_barrier_semaphore()
    for peer in peers:
        pl.semaphore_signal(barrier, inc=1, device_id=peer, device_id_type=MESH)

    place = 0
    for lane_block in range(n // LANES):
        begin = lane_block * LANES
        for row in range(begin, n, ROWS):
            share[place // piece, place % piece : place % piece + ROWS, :] = gram_ref[row : row + ROWS, begin : begin + LANES]
            place += ROWS
    for s in range(n_mem):
        share[s, piece : piece + ROWS, :] = pull_ref[...]
    pl.semaphore_wait(barrier, len(peers))

    copies = []
    for step in range(1, n_mem):
        peer = mem_peer(step)
        copies.append(
            pltpu.make_async_remote_copy(
                src_ref=share.at[peer[1]], dst_ref=mem_in.at[step - 1], send_sem=mem_send.at[step - 1],
                recv_sem=mem_recv.at[step - 1], device_id=peer, device_id_type=MESH,
            )
        )
    for copy in copies:
        copy.start()
    for copy in copies:
        copy.wait_recv()
    summed = share[mem]
    for step in range(n_mem - 1):
        summed = summed + mem_in[step]
    for s in range(n_y):
        y_out[s, :part, :] = summed[s * part : (s + 1) * part]
        y_out[s, part:, :] = summed[piece:]
    pending = copies

    copies = []
    for step in range(1, n_y):
        peer = y_peer(step)
        copies.append(
            pltpu.make_async_remote_copy(
                src_ref=y_out.at[lax.rem(y + step, n_y)], dst_ref=y_in.at[step - 1], send_sem=y_send.at[step - 1],
                recv_sem=y_recv.at[step - 1], device_id=peer, device_id_type=MESH,
            )
        )
    for copy in copies:
        copy.start()
    for copy in copies:
        copy.wait_recv()
    summed = y_out[y]
    for step in range(n_y - 1):
        summed = summed + y_in[step]
    z_in[z] = summed
    pending = pending + copies

    copies = []
    for step in range(1, n_z):
        copies.append(
            pltpu.make_async_remote_copy(
                src_ref=z_in.at[z], dst_ref=z_in.at[z], send_sem=z_send.at[step - 1],
                recv_sem=z_recv.at[step - 1], device_id=z_peer(step), device_id_type=MESH,
            )
        )
    for copy in copies:
        copy.start()
    for copy in copies:
        copy.wait_recv()
    summed = z_in[0]
    for s in range(1, n_z):
        summed = summed + z_in[s]
    pulled_ref[...] = summed[part:]
    own = pl.ds(pl.multiple_of(y * part, ROWS), part)
    total_ref[mem, own, :] = summed[:part]
    pending = pending + copies

    copies = []
    for step in range(1, n_y):
        copies.append(
            pltpu.make_async_remote_copy(
                src_ref=total_ref.at[mem, own], dst_ref=total_ref.at[mem, own], send_sem=yg_send.at[step - 1],
                recv_sem=yg_recv.at[step - 1], device_id=y_peer(step), device_id_type=MESH,
            )
        )
    for copy in copies:
        copy.start()
    for copy in copies:
        copy.wait_recv()
    pending = pending + copies
    copies = []
    for step in range(1, n_mem):
        copies.append(
            pltpu.make_async_remote_copy(
                src_ref=total_ref.at[mem], dst_ref=total_ref.at[mem], send_sem=mg_send.at[step - 1],
                recv_sem=mg_recv.at[step - 1], device_id=mem_peer(step), device_id_type=MESH,
            )
        )
    for copy in copies:
        copy.start()
    for copy in copies:
        copy.wait_recv()
    for copy in pending + copies:
        copy.wait_send()


def totals(gram_part, pull_tile, n_y, n_z):
    n = gram_part.shape[0]
    n_mem = lax.axis_size("mem")
    blocks = n // LANES
    packed = LANES * LANES * blocks * (blocks + 1) // 2 // LANES
    piece = packed // n_mem
    dma = pltpu.SemaphoreType.DMA
    part = piece // n_y
    return pl.pallas_call(
        functools.partial(total_kernel, n, n_mem, n_y, n_z),
        out_shape=(
            jax.ShapeDtypeStruct((n_mem, piece, LANES), F32),
            jax.ShapeDtypeStruct((ROWS, LANES), F32),
        ),
        in_specs=[pl.BlockSpec(memory_space=pltpu.VMEM)] * 2,
        out_specs=(pl.BlockSpec(memory_space=pltpu.VMEM),) * 2,
        scratch_shapes=[
            pltpu.VMEM((n_mem, piece + ROWS, LANES), F32),
            pltpu.VMEM((n_mem - 1, piece + ROWS, LANES), F32),
            pltpu.VMEM((n_y, part + ROWS, LANES), F32),
            pltpu.VMEM((n_y - 1, part + ROWS, LANES), F32),
            pltpu.VMEM((n_z, part + ROWS, LANES), F32),
            dma((n_mem - 1,)), dma((n_mem - 1,)), dma((n_y - 1,)), dma((n_y - 1,)), dma((n_z - 1,)), dma((n_z - 1,)),
            dma((n_y - 1,)), dma((n_y - 1,)), dma((n_mem - 1,)), dma((n_mem - 1,)),
        ],
        compiler_params=pltpu.CompilerParams(collective_id=0, has_side_effects=True),
        name="totals",
    )(gram_part, pull_tile)


def precise_dot(left, right, contract=((1,), (0,))):
    return lax.dot_general(
        left, right, (contract, ((), ())), precision=lax.Precision.HIGHEST, preferred_element_type=F32
    )


def inverse_factor_rows(tiles, group):
    tiles = list(tiles)
    extent = tiles[0].shape[1]
    lane = lax.broadcasted_iota(jnp.int32, (ROWS, extent), 1)
    sublane = lax.broadcasted_iota(jnp.int32, (ROWS, extent), 0)

    def spread(value):
        return jnp.broadcast_to(value, (ROWS, extent))

    for first in range(0, extent, group):
        home, top = first // ROWS, first % ROWS
        own = tiles[home]
        columns = [
            [spread(tile[:, first + a : first + a + 1]) for tile in tiles[home:]] for a in range(group)
        ]
        pivots = {
            (b, a): spread(columns[a][0][top + b : top + b + 1, :]) for a in range(group) for b in range(a, group)
        }
        member = (lane >= first) & (lane < first + group)
        rows = [
            jnp.where(member, jnp.where(lane == first + a, 1.0, 0.0), spread(own[top + a : top + a + 1, :]))
            for a in range(group)
        ]
        for a in range(group):
            scale = lax.rsqrt(pivots[(a, a)])
            rows[a] = rows[a] * scale
            columns[a] = [column * scale for column in columns[a]]
            below = {b: pivots[(b, a)] * scale for b in range(a + 1, group)}
            for b in range(a + 1, group):
                for c in range(a + 1, b + 1):
                    pivots[(b, c)] = pivots[(b, c)] - below[b] * below[c]
                rows[b] = rows[b] - below[b] * rows[a]
                columns[b] = [right - left * below[b] for right, left in zip(columns[b], columns[a])]
        for index in range(home, len(tiles)):
            if index == home and group == ROWS:
                fresh = own
            else:
                fresh = jnp.where(member, 0.0, tiles[index])
                for a in range(group):
                    fresh = fresh - columns[a][index - home] * rows[a]
            if index == home:
                fresh = jnp.where(sublane < top, own, fresh)
                for a in range(group):
                    fresh = jnp.where(sublane == top + a, rows[a], fresh)
            tiles[index] = fresh
    return tiles


def mixing_kernel(n, width, group, packed_ref, pull_ref, out_ref, work):
    shape = (width, width)
    row = lax.broadcasted_iota(jnp.int32, shape, 0)
    column = lax.broadcasted_iota(jnp.int32, shape, 1)
    unit = jnp.where(row == column, 1.0, 0.0)
    place = 0
    for begin in range(0, n, width):
        work[begin:n, begin : begin + width] = packed_ref[place : place + n - begin, :]
        place += n - begin
        index = begin // width
        work[n : n + 1, begin : begin + width] = pull_ref[index : index + 1, :]
    work[n + 1 :, :] = jnp.zeros((ROWS - 1, n), F32)
    for begin in range(0, n, width):
        end = begin + width
        block = work[begin:end, begin:end] + (n - 1.0) * unit
        tiles = inverse_factor_rows([block[i : i + ROWS] for i in range(0, width, ROWS)], group)
        inverse = jnp.where(column <= row, jnp.concatenate(tiles, axis=0), 0.0)
        below = precise_dot(work[end:, begin:end], inverse, ((1,), (1,)))
        if begin > 0:
            work[begin:end, :begin] = precise_dot(inverse, work[begin:end, :begin])
        work[begin:end, begin:end] = inverse
        work[end:, begin:end] = jnp.zeros((n + ROWS - end, width), F32)
        work[end:, :end] = work[end:, :end] - precise_dot(below, work[begin:end, :end])
        if end < n:
            work[end:, end:] = work[end:, end:] - precise_dot(below, below[: n - end], ((1,), (1,)))
    whole = (n, n)
    lower = lax.broadcasted_iota(jnp.int32, whole, 1) <= lax.broadcasted_iota(jnp.int32, whole, 0)
    scaled = jnp.where(lower, work[:n, :] * math.sqrt(n - 1.0), 0.0)
    out_ref[...] = (scaled - work[n : n + 1, :]).astype(jnp.bfloat16)


def mixing_rows(packed, pull_tile, n):
    return pl.pallas_call(
        functools.partial(mixing_kernel, n, LANES, ROWS),
        out_shape=jax.ShapeDtypeStruct((n, n), jnp.bfloat16),
        in_specs=[pl.BlockSpec(memory_space=pltpu.VMEM)] * 2,
        out_specs=pl.BlockSpec(memory_space=pltpu.VMEM),
        scratch_shapes=[pltpu.VMEM((n + ROWS, n), F32)],
        compiler_params=pltpu.CompilerParams(vmem_limit_bytes=24 << 20),
        name="mixing",
    )(packed, pull_tile)


def local(
    background_copies,
    measuring_span_leading_cell,
    measuring_kernel_coefficients,
    measured_readings,
    measured_error_precision,
):
    predicted_copies = background_copies.shape[0] * lax.axis_size("mem")
    sea_grid_piece = lax.all_to_all(
        background_copies, "mem", split_axis=1, concat_axis=0, tiled=True
    )
    cells_here = sea_grid_piece.shape[1]
    reach = measuring_kernel_coefficients.shape[1]
    edge_cells = jnp.transpose(sea_grid_piece[:, : reach - 1])
    outside_extension = passed_along(edge_cells, ("cells", "mem"), -1)
    predicted_centroid = jnp.sum(sea_grid_piece, axis=0, dtype=jnp.float32) / predicted_copies
    copy_anomalies = (sea_grid_piece.astype(jnp.float32) - predicted_centroid[None, :]).astype(
        jnp.bfloat16
    )
    outside_centroid = jnp.sum(outside_extension, axis=1, dtype=jnp.float32) / predicted_copies
    beyond_anomaly = (outside_extension.astype(jnp.float32) - outside_centroid[:, None]).astype(
        jnp.bfloat16
    )
    primary_lookup = operator_table(
        measuring_span_leading_cell, measuring_kernel_coefficients, 0, cells_here
    )
    rim_table = operator_table(
        measuring_span_leading_cell, measuring_kernel_coefficients, cells_here, reach - 1
    )
    projected = lax.dot_general(
        primary_lookup, copy_anomalies, (((1,), (1,)), ((), ())), preferred_element_type=jnp.float32
    )
    projected = projected + jnp.dot(rim_table, beyond_anomaly, preferred_element_type=jnp.float32)
    observed_mean = jnp.dot(
        primary_lookup.astype(jnp.float32), predicted_centroid, precision=lax.Precision.HIGHEST
    )
    observed_mean = observed_mean + jnp.dot(
        rim_table.astype(jnp.float32), outside_centroid, precision=lax.Precision.HIGHEST
    )
    root = jnp.sqrt(measured_error_precision)
    weighted = (root[:, None] * projected).astype(jnp.bfloat16)
    innovation = (root * (measured_readings - observed_mean)).astype(jnp.bfloat16)
    gram_part = lax.dot_general(
        weighted, weighted, (((0,), (0,)), ((), ())), preferred_element_type=jnp.float32
    )
    pull_part = lax.dot_general(
        innovation, weighted, (((0,), (0,)), ((), ())), preferred_element_type=jnp.float32
    )
    blocks = predicted_copies // LANES
    pull_tile = jnp.concatenate(
        [pull_part.reshape(blocks, LANES), jnp.zeros((ROWS - blocks, LANES), F32)], axis=0
    )
    n_z = lax.axis_size("cells") // N_Y
    total, pulled = totals(gram_part, pull_tile, N_Y, n_z)
    mixing_transposed = mixing_rows(total.reshape(-1, LANES), pulled, predicted_copies)
    return predicted_centroid[None, :] + lax.dot_general(
        mixing_transposed, copy_anomalies, (((1,), (0,)), ((), ())), preferred_element_type=jnp.float32
    )


def solution(mesh):
    in_specs = (
        P("mem", "cells"),
        P(("cells", "mem")),
        P(("cells", "mem"), None),
        P(("cells", "mem")),
        P(("cells", "mem")),
    )
    out_specs = P(None, ("cells", "mem"))
    return jax.shard_map(local, mesh=mesh, in_specs=in_specs, out_specs=out_specs, check_vma=False)
```

```python
import functools
import math

import jax
import jax.numpy as jnp
from jax import lax
from jax.experimental import pallas as pl
from jax.experimental.pallas import tpu as pltpu
from jax.sharding import PartitionSpec as P

F32 = jnp.float32
N_Y = 4
ROWS, LANES = 8, 128
MESH = pl.DeviceIdType.MESH


def front_kernel(n_mem, n_y, n_z, field_ref, start_ref, weight_ref, reading_ref, precision_ref,
                 total_ref, pulled_ref, anomaly_ref, mean_ref,
                 state, spread_out, table, weighted, a_out, a_in, b_out, b_in, ay_out, ay_in, bm_out, bm_in, az, bz,
                 own_sem, edge_send, edge_recv, x_send, x_recv,
                 a_sem, b_sem, ay_sem, bm_sem, az_sem, bz_sem, ag_sem, bg_sem, ah_sem, bh_sem):
    cell, mem = lax.axis_index("cells"), lax.axis_index("mem")
    n_cells = n_y * n_z
    y, z = lax.rem(cell, n_y), cell // n_y
    members = field_ref.shape[0]
    n = members * n_mem
    here = anomaly_ref.shape[1]
    wide = state.shape[1]
    edge = wide - here
    last = n_mem - 1

    def mem_peer(step):
        return (cell, lax.rem(mem + step, n_mem))

    def y_peer(step):
        return (z * n_y + lax.rem(y + step, n_y), mem)

    def z_peer(step):
        return (lax.rem(z + step, n_z) * n_y + y, mem)

    def signal(peer):
        pl.semaphore_signal(barrier, inc=1, device_id=peer, device_id_type=MESH)

    barrier = pltpu.get_barrier_semaphore()
    for step in range(1, n_mem):
        signal(mem_peer(step))
    for step in range(1, n_y):
        signal(y_peer(step))
    for step in range(1, n_z):
        signal(z_peer(step))

    @pl.when(mem == last)
    def _():
        for source in range(n_mem):
            signal((lax.rem(cell + 1, n_cells), source))

    pl.semaphore_wait(barrier, n_mem + n_y + n_z - 2)

    rows_here = pl.ds(pl.multiple_of(mem * members, members), members)

    def slab_copy(step, width):
        target = lax.rem(mem + step, n_mem)
        return pltpu.make_async_remote_copy(
            src_ref=field_ref.at[:, pl.ds(pl.multiple_of(target * here, here), width)],
            dst_ref=state.at[rows_here, pl.ds(0, width)],
            send_sem=x_send.at[step - 1], recv_sem=x_recv.at[step - 1],
            device_id=mem_peer(step), device_id_type=MESH,
        )

    def arrival(step, width):
        source = lax.rem(mem + n_mem - step, n_mem)
        rows = pl.ds(pl.multiple_of(source * members, members), members)
        return pltpu.make_async_remote_copy(
            src_ref=field_ref.at[:, pl.ds(0, width)], dst_ref=state.at[rows, pl.ds(0, width)],
            send_sem=x_send.at[step - 1], recv_sem=x_recv.at[step - 1],
            device_id=mem_peer(step), device_id_type=MESH,
        )

    def own_copy(width):
        return pltpu.make_async_copy(
            field_ref.at[:, pl.ds(pl.multiple_of(mem * here, here), width)],
            state.at[rows_here, pl.ds(0, width)], own_sem,
        )

    def edge_copy(source):
        rows = pl.ds(pl.multiple_of(source * members, members), members)
        return pltpu.make_async_remote_copy(
            src_ref=field_ref.at[:, pl.ds(0, edge)], dst_ref=state.at[rows, pl.ds(here, edge)],
            send_sem=edge_send, recv_sem=edge_recv.at[source],
            device_id=(lax.rem(cell + n_cells - 1, n_cells), last), device_id_type=MESH,
        )

    for step in range(1, n_mem):
        target = lax.rem(mem + step, n_mem)

        @pl.when(target != last)
        def _(step=step):
            slab_copy(step, wide).start()

        @pl.when(target == last)
        def _(step=step):
            slab_copy(step, here).start()

    edge_copy(mem).start()

    @pl.when(mem != last)
    def _():
        own_copy(wide).start()

    @pl.when(mem == last)
    def _():
        own_copy(here).start()

    start = start_ref[...]
    taps = [weight_ref[j : j + 1, :].astype(F32) for j in range(weight_ref.shape[0])]
    chunk = 64

    @pl.loop(0, wide // chunk)
    def _(index):
        first = pl.multiple_of(index * chunk, chunk)
        ahead = lax.broadcasted_iota(jnp.int32, (chunk, start.shape[1]), 0) + first - start
        block = jnp.zeros(ahead.shape, F32)
        for j, tap in enumerate(taps):
            block = jnp.where(ahead == j, tap, block)
        table[pl.ds(first, chunk), :] = block.astype(jnp.bfloat16)

    @pl.when(mem != last)
    def _():
        own_copy(wide).wait()
        for step in range(1, n_mem):
            arrival(step, wide).wait_recv()

    @pl.when(mem == last)
    def _():
        own_copy(here).wait()
        for step in range(1, n_mem):
            arrival(step, here).wait_recv()
        for source in range(n_mem):
            edge_copy(source).wait_recv()

    step_rows = 64

    def add_rows(index, total):
        first = pl.multiple_of(index * step_rows, step_rows)
        return total + jnp.sum(state[pl.ds(first, step_rows), :].astype(F32).reshape(step_rows // ROWS, ROWS, wide), axis=0)

    sums = lax.fori_loop(0, n // step_rows, add_rows, jnp.zeros((ROWS, wide), F32))
    mean = jnp.sum(sums, axis=0, keepdims=True) / n
    mean_ref[...] = mean[:, :here]

    @pl.loop(0, n // step_rows)
    def _(index):
        rows = pl.ds(pl.multiple_of(index * step_rows, step_rows), step_rows)
        away = (state[rows, :].astype(F32) - mean).astype(jnp.bfloat16)
        spread_out[rows, :] = away
        anomaly_ref[rows, :] = away[:, :here]

    high = mean.astype(jnp.bfloat16)
    rest = mean - high.astype(F32)
    middle = rest.astype(jnp.bfloat16)
    small = (rest - middle.astype(F32)).astype(jnp.bfloat16)
    spread_out[n:, :] = jnp.concatenate([high, middle, small, jnp.zeros((13, wide), jnp.bfloat16)], axis=0)
    projected = jnp.dot(spread_out[...], table[...], preferred_element_type=F32)
    root = jnp.sqrt(precision_ref[...])
    observed = projected[n : n + 1] + (projected[n + 1 : n + 2] + projected[n + 2 : n + 3])
    innovation = (root * (reading_ref[...] - observed)).astype(jnp.bfloat16)
    weighted[:n, :] = (root * projected[:n]).astype(jnp.bfloat16)
    weighted[n:, :] = jnp.concatenate([innovation, jnp.zeros((15, innovation.shape[1]), jnp.bfloat16)], axis=0)

    a_piece = a_out.shape[1] - ROWS
    b_piece = b_out.shape[1]
    a_rows = n_mem * a_piece
    place = 0
    pull = []
    for begin in range(0, n, LANES):
        product = lax.dot_general(
            weighted[begin:, :], weighted[begin : begin + LANES, :], (((1,), (1,)), ((), ())), preferred_element_type=F32
        )
        pull.append(product[n - begin : n - begin + 1])
        for row in range(0, n - begin, ROWS):
            tile = product[row : row + ROWS]
            if place < a_rows:
                a_out[place // a_piece, place % a_piece : place % a_piece + ROWS, :] = tile
            else:
                spot = place - a_rows
                b_out[spot // b_piece, spot % b_piece : spot % b_piece + ROWS, :] = tile
            place += ROWS
    pull_tile = jnp.concatenate(pull + [jnp.zeros((ROWS - len(pull), LANES), F32)], axis=0)
    for s in range(n_mem):
        a_out[s, a_piece:, :] = pull_tile

    def begin_all(sources, target, peer, sems, count):
        copies = [
            pltpu.make_async_remote_copy(
                src_ref=sources(step), dst_ref=target(step), send_sem=sems.at[0, step - 1], recv_sem=sems.at[1, step - 1],
                device_id=peer(step), device_id_type=MESH,
            )
            for step in range(1, count)
        ]
        for copy in copies:
            copy.start()
        pending.extend(copies)
        return copies

    def arrived(copies):
        for copy in copies:
            copy.wait_recv()

    pending = []
    a_part = az.shape[1] - ROWS
    b_part = bz.shape[1]
    a1 = begin_all(lambda s: a_out.at[lax.rem(mem + s, n_mem)], lambda s: a_in.at[s - 1], mem_peer, a_sem, n_mem)
    b1 = begin_all(lambda s: b_out.at[lax.rem(y + s, n_y)], lambda s: b_in.at[s - 1], y_peer, b_sem, n_y)
    arrived(a1)
    summed = a_out[mem]
    for s in range(n_mem - 1):
        summed = summed + a_in[s]
    for s in range(n_y):
        ay_out[s, :a_part, :] = summed[s * a_part : (s + 1) * a_part]
        ay_out[s, a_part:, :] = summed[a_piece:]
    a2 = begin_all(lambda s: ay_out.at[lax.rem(y + s, n_y)], lambda s: ay_in.at[s - 1], y_peer, ay_sem, n_y)
    arrived(b1)
    summed = b_out[y]
    for s in range(n_y - 1):
        summed = summed + b_in[s]
    for s in range(n_mem):
        bm_out[s] = summed[s * b_part : (s + 1) * b_part]
    b2 = begin_all(lambda s: bm_out.at[lax.rem(mem + s, n_mem)], lambda s: bm_in.at[s - 1], mem_peer, bm_sem, n_mem)
    arrived(a2)
    summed = ay_out[y]
    for s in range(n_y - 1):
        summed = summed + ay_in[s]
    az[z] = summed
    a3 = begin_all(lambda s: az.at[z], lambda s: az.at[z], z_peer, az_sem, n_z)
    arrived(b2)
    summed = bm_out[mem]
    for s in range(n_mem - 1):
        summed = summed + bm_in[s]
    bz[z] = summed
    b3 = begin_all(lambda s: bz.at[z], lambda s: bz.at[z], z_peer, bz_sem, n_z)
    arrived(a3)
    summed = az[0]
    for s in range(1, n_z):
        summed = summed + az[s]
    pulled_ref[...] = summed[a_part:]
    a_slab = pl.ds(pl.multiple_of(mem * a_piece, a_piece), a_piece)
    a_own = pl.ds(pl.multiple_of(mem * a_piece + y * a_part, ROWS), a_part)
    total_ref[a_own, :] = summed[:a_part]
    a4 = begin_all(lambda s: total_ref.at[a_own], lambda s: total_ref.at[a_own], y_peer, ag_sem, n_y)
    arrived(b3)
    summed = bz[0]
    for s in range(1, n_z):
        summed = summed + bz[s]
    b_slab = pl.ds(pl.multiple_of(a_rows + y * b_piece, ROWS), b_piece)
    b_own = pl.ds(pl.multiple_of(a_rows + y * b_piece + mem * b_part, ROWS), b_part)
    total_ref[b_own, :] = summed
    b4 = begin_all(lambda s: total_ref.at[b_own], lambda s: total_ref.at[b_own], mem_peer, bg_sem, n_mem)
    arrived(a4)
    a5 = begin_all(lambda s: total_ref.at[a_slab], lambda s: total_ref.at[a_slab], mem_peer, ah_sem, n_mem)
    arrived(b4)
    b5 = begin_all(lambda s: total_ref.at[b_slab], lambda s: total_ref.at[b_slab], y_peer, bh_sem, n_y)
    arrived(a5)
    arrived(b5)
    for copy in pending:
        copy.wait_send()
    edge_copy(mem).wait_send()
    for step in range(1, n_mem):
        target = lax.rem(mem + step, n_mem)

        @pl.when(target != last)
        def _(step=step):
            slab_copy(step, wide).wait_send()

        @pl.when(target == last)
        def _(step=step):
            slab_copy(step, here).wait_send()


def front(field, start, weights, readings, precision, n_y, n_z):
    members, slab = field.shape
    n_mem = lax.axis_size("mem")
    n, here = members * n_mem, slab // n_mem
    observations = start.shape[1]
    blocks = n // LANES
    packed = LANES * blocks * (blocks + 1) // 2
    a_part = packed * 3 // 5 // (n_mem * n_y)
    b_part = (packed - a_part * n_mem * n_y) // (n_mem * n_y)
    a_piece, b_piece = a_part * n_y, b_part * n_mem
    dma = pltpu.SemaphoreType.DMA
    vmem = pl.BlockSpec(memory_space=pltpu.VMEM)
    bf16 = jnp.bfloat16
    return pl.pallas_call(
        functools.partial(front_kernel, n_mem, n_y, n_z),
        out_shape=(
            jax.ShapeDtypeStruct((packed, LANES), F32),
            jax.ShapeDtypeStruct((ROWS, LANES), F32),
            jax.ShapeDtypeStruct((n, here), bf16),
            jax.ShapeDtypeStruct((1, here), F32),
        ),
        in_specs=[pl.BlockSpec(memory_space=pl.ANY)] + [vmem] * 4,
        out_specs=(vmem,) * 4,
        scratch_shapes=[
            pltpu.VMEM((n, here + LANES), bf16),
            pltpu.VMEM((n + 16, here + LANES), bf16),
            pltpu.VMEM((here + LANES, observations), bf16),
            pltpu.VMEM((n + 16, observations), bf16),
            pltpu.VMEM((n_mem, a_piece + ROWS, LANES), F32),
            pltpu.VMEM((n_mem - 1, a_piece + ROWS, LANES), F32),
            pltpu.VMEM((n_y, b_piece, LANES), F32),
            pltpu.VMEM((n_y - 1, b_piece, LANES), F32),
            pltpu.VMEM((n_y, a_part + ROWS, LANES), F32),
            pltpu.VMEM((n_y - 1, a_part + ROWS, LANES), F32),
            pltpu.VMEM((n_mem, b_part, LANES), F32),
            pltpu.VMEM((n_mem - 1, b_part, LANES), F32),
            pltpu.VMEM((n_z, a_part + ROWS, LANES), F32),
            pltpu.VMEM((n_z, b_part, LANES), F32),
            dma, dma, dma((n_mem,)), dma((n_mem - 1,)), dma((n_mem - 1,)),
            dma((2, n_mem - 1)), dma((2, n_y - 1)), dma((2, n_y - 1)), dma((2, n_mem - 1)),
            dma((2, n_z - 1)), dma((2, n_z - 1)),
            dma((2, n_y - 1)), dma((2, n_mem - 1)), dma((2, n_mem - 1)), dma((2, n_y - 1)),
        ],
        compiler_params=pltpu.CompilerParams(collective_id=0, has_side_effects=True, vmem_limit_bytes=20 << 20),
        name="front",
    )(field, start, weights, readings, precision)

def precise_dot(left, right, contract=((1,), (0,))):
    return lax.dot_general(
        left, right, (contract, ((), ())), precision=lax.Precision.HIGHEST, preferred_element_type=F32
    )


def inverse_factor_rows(tiles, group):
    tiles = list(tiles)
    extent = tiles[0].shape[1]
    lane = lax.broadcasted_iota(jnp.int32, (ROWS, extent), 1)
    sublane = lax.broadcasted_iota(jnp.int32, (ROWS, extent), 0)

    def spread(value):
        return jnp.broadcast_to(value, (ROWS, extent))

    for first in range(0, extent, group):
        home, top = first // ROWS, first % ROWS
        own = tiles[home]
        columns = [
            [spread(tile[:, first + a : first + a + 1]) for tile in tiles[home:]] for a in range(group)
        ]
        pivots = {
            (b, a): spread(columns[a][0][top + b : top + b + 1, :]) for a in range(group) for b in range(a, group)
        }
        member = (lane >= first) & (lane < first + group)
        rows = [
            jnp.where(member, jnp.where(lane == first + a, 1.0, 0.0), spread(own[top + a : top + a + 1, :]))
            for a in range(group)
        ]
        for a in range(group):
            scale = lax.rsqrt(pivots[(a, a)])
            rows[a] = rows[a] * scale
            columns[a] = [column * scale for column in columns[a]]
            below = {b: pivots[(b, a)] * scale for b in range(a + 1, group)}
            for b in range(a + 1, group):
                for c in range(a + 1, b + 1):
                    pivots[(b, c)] = pivots[(b, c)] - below[b] * below[c]
                rows[b] = rows[b] - below[b] * rows[a]
                columns[b] = [right - left * below[b] for right, left in zip(columns[b], columns[a])]
        for index in range(home, len(tiles)):
            if index == home and group == ROWS:
                fresh = own
            else:
                fresh = jnp.where(member, 0.0, tiles[index])
                for a in range(group):
                    fresh = fresh - columns[a][index - home] * rows[a]
            if index == home:
                fresh = jnp.where(sublane < top, own, fresh)
                for a in range(group):
                    fresh = jnp.where(sublane == top + a, rows[a], fresh)
            tiles[index] = fresh
    return tiles


def mixing_kernel(n, width, group, packed_ref, pull_ref, out_ref, work):
    shape = (width, width)
    row = lax.broadcasted_iota(jnp.int32, shape, 0)
    column = lax.broadcasted_iota(jnp.int32, shape, 1)
    unit = jnp.where(row == column, 1.0, 0.0)
    place = 0
    for begin in range(0, n, width):
        work[begin:n, begin : begin + width] = packed_ref[place : place + n - begin, :]
        place += n - begin
        index = begin // width
        work[n : n + 1, begin : begin + width] = pull_ref[index : index + 1, :]
    work[n + 1 :, :] = jnp.zeros((ROWS - 1, n), F32)
    for begin in range(0, n, width):
        end = begin + width
        block = work[begin:end, begin:end] + (n - 1.0) * unit
        tiles = inverse_factor_rows([block[i : i + ROWS] for i in range(0, width, ROWS)], group)
        inverse = jnp.where(column <= row, jnp.concatenate(tiles, axis=0), 0.0)
        below = precise_dot(work[end:, begin:end], inverse, ((1,), (1,)))
        if begin > 0:
            work[begin:end, :begin] = precise_dot(inverse, work[begin:end, :begin])
        work[begin:end, begin:end] = inverse
        work[end:, begin:end] = jnp.zeros((n + ROWS - end, width), F32)
        work[end:, :end] = work[end:, :end] - precise_dot(below, work[begin:end, :end])
        if end < n:
            work[end:, end:] = work[end:, end:] - precise_dot(below, below[: n - end], ((1,), (1,)))
    whole = (n, n)
    lower = lax.broadcasted_iota(jnp.int32, whole, 1) <= lax.broadcasted_iota(jnp.int32, whole, 0)
    scaled = jnp.where(lower, work[:n, :] * math.sqrt(n - 1.0), 0.0)
    out_ref[...] = (scaled - work[n : n + 1, :]).astype(jnp.bfloat16)


def mixing_rows(packed, pull_tile, n):
    return pl.pallas_call(
        functools.partial(mixing_kernel, n, LANES, ROWS),
        out_shape=jax.ShapeDtypeStruct((n, n), jnp.bfloat16),
        in_specs=[pl.BlockSpec(memory_space=pltpu.VMEM)] * 2,
        out_specs=pl.BlockSpec(memory_space=pltpu.VMEM),
        scratch_shapes=[pltpu.VMEM((n + ROWS, n), F32)],
        compiler_params=pltpu.CompilerParams(vmem_limit_bytes=24 << 20),
        name="mixing",
    )(packed, pull_tile)


def local(
    background_copies,
    measuring_span_leading_cell,
    measuring_kernel_coefficients,
    measured_readings,
    measured_error_precision,
):
    predicted_copies = background_copies.shape[0] * lax.axis_size("mem")
    total, pulled, copy_anomalies, predicted_centroid = front(
        background_copies,
        measuring_span_leading_cell[None, :],
        jnp.transpose(measuring_kernel_coefficients),
        measured_readings[None, :],
        measured_error_precision[None, :],
        N_Y,
        lax.axis_size("cells") // N_Y,
    )
    mixing_transposed = mixing_rows(total, pulled, predicted_copies)
    return predicted_centroid + lax.dot_general(
        mixing_transposed, copy_anomalies, (((1,), (0,)), ((), ())), preferred_element_type=jnp.float32
    )


def solution(mesh):
    in_specs = (
        P("mem", "cells"),
        P(("cells", "mem")),
        P(("cells", "mem"), None),
        P(("cells", "mem")),
        P(("cells", "mem")),
    )
    out_specs = P(None, ("cells", "mem"))
    return jax.shard_map(local, mesh=mesh, in_specs=in_specs, out_specs=out_specs, check_vma=False)
```

```python
import functools
import math

import jax
import jax.numpy as jnp
from jax import lax
from jax.experimental import pallas as pl
from jax.experimental.pallas import tpu as pltpu
from jax.sharding import PartitionSpec as P

F32 = jnp.float32
N_Y = 4
ROWS, LANES = 8, 128
MESH = pl.DeviceIdType.MESH


def front_kernel(n_mem, n_y, n_z, field_ref, start_hbm, weight_hbm, reading_hbm, precision_hbm,
                 total_ref, pulled_ref, anomaly_ref, mean_ref,
                 start_ref, weight_ref, reading_ref, precision_ref, state, spread_out, table, weighted, a_out, a_in, b_out, b_in, ay_out, ay_in, bm_out, bm_in, az, bz,
                 small_sem, own_sem, edge_send, edge_recv, x_send, x_recv,
                 a_sem, b_sem, ay_sem, bm_sem, az_sem, bz_sem, ag_sem, bg_sem, ah_sem, bh_sem):
    cell, mem = lax.axis_index("cells"), lax.axis_index("mem")
    n_cells = n_y * n_z
    y, z = lax.rem(cell, n_y), cell // n_y
    members = field_ref.shape[0]
    n = members * n_mem
    here = anomaly_ref.shape[1]
    wide = state.shape[1]
    edge = wide - here
    last = n_mem - 1

    def mem_peer(step):
        return (cell, lax.rem(mem + step, n_mem))

    def y_peer(step):
        return (z * n_y + lax.rem(y + step, n_y), mem)

    def z_peer(step):
        return (lax.rem(z + step, n_z) * n_y + y, mem)

    def signal(peer):
        pl.semaphore_signal(barrier, inc=1, device_id=peer, device_id_type=MESH)

    small = [
        pltpu.make_async_copy(source, target, small_sem.at[index])
        for index, (source, target) in enumerate(
            ((start_hbm, start_ref), (weight_hbm, weight_ref), (reading_hbm, reading_ref), (precision_hbm, precision_ref))
        )
    ]
    for copy in small:
        copy.start()

    barrier = pltpu.get_barrier_semaphore()
    for step in range(1, n_mem):
        signal(mem_peer(step))
    for step in range(1, n_y):
        signal(y_peer(step))
    for step in range(1, n_z):
        signal(z_peer(step))

    @pl.when(mem == last)
    def _():
        for source in range(n_mem):
            signal((lax.rem(cell + 1, n_cells), source))

    rows_here = pl.ds(pl.multiple_of(mem * members, members), members)

    def own_copy(width):
        return pltpu.make_async_copy(
            field_ref.at[:, pl.ds(pl.multiple_of(mem * here, here), width)],
            state.at[rows_here, pl.ds(0, width)], own_sem,
        )

    @pl.when(mem != last)
    def _():
        own_copy(wide).start()

    @pl.when(mem == last)
    def _():
        own_copy(here).start()

    pl.semaphore_wait(barrier, n_mem + n_y + n_z - 2)

    def slab_copy(step, width):
        target = lax.rem(mem + step, n_mem)
        return pltpu.make_async_remote_copy(
            src_ref=field_ref.at[:, pl.ds(pl.multiple_of(target * here, here), width)],
            dst_ref=state.at[rows_here, pl.ds(0, width)],
            send_sem=x_send.at[step - 1], recv_sem=x_recv.at[step - 1],
            device_id=mem_peer(step), device_id_type=MESH,
        )

    def arrival(step, width):
        source = lax.rem(mem + n_mem - step, n_mem)
        rows = pl.ds(pl.multiple_of(source * members, members), members)
        return pltpu.make_async_remote_copy(
            src_ref=field_ref.at[:, pl.ds(0, width)], dst_ref=state.at[rows, pl.ds(0, width)],
            send_sem=x_send.at[step - 1], recv_sem=x_recv.at[step - 1],
            device_id=mem_peer(step), device_id_type=MESH,
        )

    def edge_copy(source):
        rows = pl.ds(pl.multiple_of(source * members, members), members)
        return pltpu.make_async_remote_copy(
            src_ref=field_ref.at[:, pl.ds(0, edge)], dst_ref=state.at[rows, pl.ds(here, edge)],
            send_sem=edge_send, recv_sem=edge_recv.at[source],
            device_id=(lax.rem(cell + n_cells - 1, n_cells), last), device_id_type=MESH,
        )

    for step in range(1, n_mem):
        target = lax.rem(mem + step, n_mem)

        @pl.when(target != last)
        def _(step=step):
            slab_copy(step, wide).start()

        @pl.when(target == last)
        def _(step=step):
            slab_copy(step, here).start()

    edge_copy(mem).start()

    for copy in small:
        copy.wait()
    start = start_ref[...]
    taps = [weight_ref[j : j + 1, :].astype(F32) for j in range(weight_ref.shape[0])]
    chunk = 64

    @pl.loop(0, wide // chunk)
    def _(index):
        first = pl.multiple_of(index * chunk, chunk)
        ahead = lax.broadcasted_iota(jnp.int32, (chunk, start.shape[1]), 0) + first - start
        block = jnp.zeros(ahead.shape, F32)
        for j, tap in enumerate(taps):
            block = jnp.where(ahead == j, tap, block)
        table[pl.ds(first, chunk), :] = block.astype(jnp.bfloat16)

    @pl.when(mem != last)
    def _():
        own_copy(wide).wait()
        for step in range(1, n_mem):
            arrival(step, wide).wait_recv()

    @pl.when(mem == last)
    def _():
        own_copy(here).wait()
        for step in range(1, n_mem):
            arrival(step, here).wait_recv()
        for source in range(n_mem):
            edge_copy(source).wait_recv()

    step_rows = 64

    def add_rows(index, total):
        first = pl.multiple_of(index * step_rows, step_rows)
        return total + jnp.sum(state[pl.ds(first, step_rows), :].astype(F32).reshape(step_rows // ROWS, ROWS, wide), axis=0)

    sums = lax.fori_loop(0, n // step_rows, add_rows, jnp.zeros((ROWS, wide), F32))
    mean = jnp.sum(sums, axis=0, keepdims=True) / n
    mean_ref[...] = mean[:, :here]

    @pl.loop(0, n // step_rows)
    def _(index):
        rows = pl.ds(pl.multiple_of(index * step_rows, step_rows), step_rows)
        away = (state[rows, :].astype(F32) - mean).astype(jnp.bfloat16)
        spread_out[rows, :] = away
        anomaly_ref[rows, :] = away[:, :here]

    high = mean.astype(jnp.bfloat16)
    rest = mean - high.astype(F32)
    middle = rest.astype(jnp.bfloat16)
    small = (rest - middle.astype(F32)).astype(jnp.bfloat16)
    spread_out[n:, :] = jnp.concatenate([high, middle, small, jnp.zeros((13, wide), jnp.bfloat16)], axis=0)
    projected = jnp.dot(spread_out[...], table[...], preferred_element_type=F32)
    root = jnp.sqrt(precision_ref[...])
    observed = projected[n : n + 1] + (projected[n + 1 : n + 2] + projected[n + 2 : n + 3])
    innovation = (root * (reading_ref[...] - observed)).astype(jnp.bfloat16)
    weighted[:n, :] = (root * projected[:n]).astype(jnp.bfloat16)
    weighted[n:, :] = jnp.concatenate([innovation, jnp.zeros((15, innovation.shape[1]), jnp.bfloat16)], axis=0)

    a_piece = a_out.shape[1] - ROWS
    b_piece = b_out.shape[1]
    a_rows = n_mem * a_piece
    place = 0
    pull = []
    for begin in range(0, n, LANES):
        product = lax.dot_general(
            weighted[begin:, :], weighted[begin : begin + LANES, :], (((1,), (1,)), ((), ())), preferred_element_type=F32
        )
        pull.append(product[n - begin : n - begin + 1])
        for row in range(0, n - begin, ROWS):
            tile = product[row : row + ROWS]
            if place < a_rows:
                a_out[place // a_piece, place % a_piece : place % a_piece + ROWS, :] = tile
            else:
                spot = place - a_rows
                b_out[spot // b_piece, spot % b_piece : spot % b_piece + ROWS, :] = tile
            place += ROWS
    pull_tile = jnp.concatenate(pull + [jnp.zeros((ROWS - len(pull), LANES), F32)], axis=0)
    for s in range(n_mem):
        a_out[s, a_piece:, :] = pull_tile

    def begin_all(sources, target, peer, sems, count):
        copies = [
            pltpu.make_async_remote_copy(
                src_ref=sources(step), dst_ref=target(step), send_sem=sems.at[0, step - 1], recv_sem=sems.at[1, step - 1],
                device_id=peer(step), device_id_type=MESH,
            )
            for step in range(1, count)
        ]
        for copy in copies:
            copy.start()
        pending.extend(copies)
        return copies

    def arrived(copies):
        for copy in copies:
            copy.wait_recv()

    pending = []
    a_part = az.shape[1] - ROWS
    b_part = bz.shape[1]
    a1 = begin_all(lambda s: a_out.at[lax.rem(mem + s, n_mem)], lambda s: a_in.at[s - 1], mem_peer, a_sem, n_mem)
    b1 = begin_all(lambda s: b_out.at[lax.rem(y + s, n_y)], lambda s: b_in.at[s - 1], y_peer, b_sem, n_y)
    arrived(a1)
    summed = a_out[mem]
    for s in range(n_mem - 1):
        summed = summed + a_in[s]
    for s in range(n_y):
        ay_out[s, :a_part, :] = summed[s * a_part : (s + 1) * a_part]
        ay_out[s, a_part:, :] = summed[a_piece:]
    a2 = begin_all(lambda s: ay_out.at[lax.rem(y + s, n_y)], lambda s: ay_in.at[s - 1], y_peer, ay_sem, n_y)
    arrived(b1)
    summed = b_out[y]
    for s in range(n_y - 1):
        summed = summed + b_in[s]
    for s in range(n_mem):
        bm_out[s] = summed[s * b_part : (s + 1) * b_part]
    b2 = begin_all(lambda s: bm_out.at[lax.rem(mem + s, n_mem)], lambda s: bm_in.at[s - 1], mem_peer, bm_sem, n_mem)
    arrived(a2)
    summed = ay_out[y]
    for s in range(n_y - 1):
        summed = summed + ay_in[s]
    az[z] = summed
    a3 = begin_all(lambda s: az.at[z], lambda s: az.at[z], z_peer, az_sem, n_z)
    arrived(b2)
    summed = bm_out[mem]
    for s in range(n_mem - 1):
        summed = summed + bm_in[s]
    bz[z] = summed
    b3 = begin_all(lambda s: bz.at[z], lambda s: bz.at[z], z_peer, bz_sem, n_z)
    arrived(a3)
    summed = az[0]
    for s in range(1, n_z):
        summed = summed + az[s]
    pulled_ref[...] = summed[a_part:]
    a_slab = pl.ds(pl.multiple_of(mem * a_piece, a_piece), a_piece)
    a_own = pl.ds(pl.multiple_of(mem * a_piece + y * a_part, ROWS), a_part)
    total_ref[a_own, :] = summed[:a_part]
    a4 = begin_all(lambda s: total_ref.at[a_own], lambda s: total_ref.at[a_own], y_peer, ag_sem, n_y)
    arrived(b3)
    summed = bz[0]
    for s in range(1, n_z):
        summed = summed + bz[s]
    b_slab = pl.ds(pl.multiple_of(a_rows + y * b_piece, ROWS), b_piece)
    b_own = pl.ds(pl.multiple_of(a_rows + y * b_piece + mem * b_part, ROWS), b_part)
    total_ref[b_own, :] = summed
    b4 = begin_all(lambda s: total_ref.at[b_own], lambda s: total_ref.at[b_own], mem_peer, bg_sem, n_mem)
    arrived(a4)
    a5 = begin_all(lambda s: total_ref.at[a_slab], lambda s: total_ref.at[a_slab], mem_peer, ah_sem, n_mem)
    arrived(b4)
    b5 = begin_all(lambda s: total_ref.at[b_slab], lambda s: total_ref.at[b_slab], y_peer, bh_sem, n_y)
    arrived(a5)
    arrived(b5)
    for copy in pending:
        copy.wait_send()
    edge_copy(mem).wait_send()
    for step in range(1, n_mem):
        target = lax.rem(mem + step, n_mem)

        @pl.when(target != last)
        def _(step=step):
            slab_copy(step, wide).wait_send()

        @pl.when(target == last)
        def _(step=step):
            slab_copy(step, here).wait_send()


def front(field, start, weights, readings, precision, n_y, n_z):
    members, slab = field.shape
    n_mem = lax.axis_size("mem")
    n, here = members * n_mem, slab // n_mem
    observations = start.shape[1]
    blocks = n // LANES
    packed = LANES * blocks * (blocks + 1) // 2
    a_part = packed * 3 // 5 // (n_mem * n_y)
    b_part = (packed - a_part * n_mem * n_y) // (n_mem * n_y)
    a_piece, b_piece = a_part * n_y, b_part * n_mem
    dma = pltpu.SemaphoreType.DMA
    vmem = pl.BlockSpec(memory_space=pltpu.VMEM)
    bf16 = jnp.bfloat16
    return pl.pallas_call(
        functools.partial(front_kernel, n_mem, n_y, n_z),
        out_shape=(
            jax.ShapeDtypeStruct((packed, LANES), F32),
            jax.ShapeDtypeStruct((ROWS, LANES), F32),
            jax.ShapeDtypeStruct((n, here), bf16),
            jax.ShapeDtypeStruct((1, here), F32),
        ),
        in_specs=[pl.BlockSpec(memory_space=pltpu.HBM)] * 5,
        out_specs=(vmem,) * 4,
        scratch_shapes=[
            pltpu.VMEM(start.shape, start.dtype),
            pltpu.VMEM(weights.shape, weights.dtype),
            pltpu.VMEM(readings.shape, readings.dtype),
            pltpu.VMEM(precision.shape, precision.dtype),
            pltpu.VMEM((n, here + LANES), bf16),
            pltpu.VMEM((n + 16, here + LANES), bf16),
            pltpu.VMEM((here + LANES, observations), bf16),
            pltpu.VMEM((n + 16, observations), bf16),
            pltpu.VMEM((n_mem, a_piece + ROWS, LANES), F32),
            pltpu.VMEM((n_mem - 1, a_piece + ROWS, LANES), F32),
            pltpu.VMEM((n_y, b_piece, LANES), F32),
            pltpu.VMEM((n_y - 1, b_piece, LANES), F32),
            pltpu.VMEM((n_y, a_part + ROWS, LANES), F32),
            pltpu.VMEM((n_y - 1, a_part + ROWS, LANES), F32),
            pltpu.VMEM((n_mem, b_part, LANES), F32),
            pltpu.VMEM((n_mem - 1, b_part, LANES), F32),
            pltpu.VMEM((n_z, a_part + ROWS, LANES), F32),
            pltpu.VMEM((n_z, b_part, LANES), F32),
            dma((4,)), dma, dma, dma((n_mem,)), dma((n_mem - 1,)), dma((n_mem - 1,)),
            dma((2, n_mem - 1)), dma((2, n_y - 1)), dma((2, n_y - 1)), dma((2, n_mem - 1)),
            dma((2, n_z - 1)), dma((2, n_z - 1)),
            dma((2, n_y - 1)), dma((2, n_mem - 1)), dma((2, n_mem - 1)), dma((2, n_y - 1)),
        ],
        compiler_params=pltpu.CompilerParams(collective_id=0, has_side_effects=True, vmem_limit_bytes=20 << 20),
        name="front",
    )(*(pltpu.with_memory_space_constraint(x, pltpu.HBM) for x in (field, start, weights, readings, precision)))

def precise_dot(left, right, contract=((1,), (0,))):
    return lax.dot_general(
        left, right, (contract, ((), ())), precision=lax.Precision.HIGHEST, preferred_element_type=F32
    )


def inverse_factor_rows(tiles, panel, ahead):
    tiles = list(tiles)
    count = len(tiles)
    extent = tiles[0].shape[1]
    lane = lax.broadcasted_iota(jnp.int32, (ROWS, extent), 1)
    sublane = lax.broadcasted_iota(jnp.int32, (ROWS, extent), 0)

    def spread(value):
        return jnp.broadcast_to(value, (ROWS, extent))

    def pick(tile, position):
        return jnp.take_along_axis(tile, jnp.full((ROWS, extent), position, jnp.int32), axis=1)

    for home in range(count):
        first = home * ROWS
        panel_end = min((home // panel + 1) * panel, count)
        near_end = min(panel_end + ahead, count)
        own = tiles[home]
        lanes = [pick(own, first + a) for a in range(ROWS)]
        pivots = {(b, a): spread(lanes[a][b : b + 1, :]) for a in range(ROWS) for b in range(a, ROWS)}
        member = (lane >= first) & (lane < first + ROWS)
        rows = [
            jnp.where(member, jnp.where(lane == first + a, 1.0, 0.0), spread(own[a : a + 1, :])) for a in range(ROWS)
        ]
        scales = []
        for a in range(ROWS):
            scale = lax.rsqrt(pivots[(a, a)])
            scales.append(scale)
            rows[a] = rows[a] * scale
            for b in range(a + 1, ROWS):
                pivots[(b, a)] = pivots[(b, a)] * scale
            for b in range(a + 1, ROWS):
                for c in range(a + 1, b + 1):
                    pivots[(b, c)] = pivots[(b, c)] - pivots[(b, a)] * pivots[(c, a)]
                rows[b] = rows[b] - pivots[(b, a)] * rows[a]
        fresh = rows[0]
        for a in range(1, ROWS):
            fresh = jnp.where(sublane == a, rows[a], fresh)
        tiles[home] = fresh
        solved = list(rows)
        for a in range(ROWS - 1, -1, -1):
            solved[a] = solved[a] * scales[a]
            for b in range(a):
                solved[b] = solved[b] - pivots[(a, b)] * solved[a]
        for index in range(home + 1, near_end):
            tile = tiles[index]
            fresh = jnp.where(member, 0.0, tile)
            for a in range(ROWS):
                fresh = fresh - pick(tile, first + a) * solved[a]
            tiles[index] = fresh
        if home + 1 == panel_end and near_end < count:
            begin = (home // panel) * panel
            done = tiles[begin:panel_end]
            masked = [
                jnp.where((lane >= (begin + i + 1) * ROWS) & (lane < panel_end * ROWS), 0.0, tile)
                for i, tile in enumerate(done)
            ]
            change = precise_dot(jnp.concatenate(done, axis=0), jnp.concatenate(masked, axis=0), ((0,), (0,)))
            inside = (lane >= begin * ROWS) & (lane < panel_end * ROWS)
            for index in range(near_end, count):
                tiles[index] = jnp.where(inside, 0.0, tiles[index]) - change[index * ROWS : (index + 1) * ROWS]
    return tiles


def analysis_kernel(n, width, packed_ref, pull_ref, anomaly_ref, mean_ref, out_hbm, work, out, sems):
    shape = (width, width)
    row = lax.broadcasted_iota(jnp.int32, shape, 0)
    column = lax.broadcasted_iota(jnp.int32, shape, 1)
    unit = jnp.where(row == column, 1.0, 0.0)
    place = 0
    for begin in range(0, n, width):
        work[begin:n, begin : begin + width] = packed_ref[place : place + n - begin, :]
        place += n - begin
        index = begin // width
        work[n : n + 1, begin : begin + width] = pull_ref[index : index + 1, :]
    work[n + 1 :, :] = jnp.zeros((ROWS - 1, n), F32)
    diagonal = work[:width, :width]
    for begin in range(0, n, width):
        end = begin + width
        block = diagonal + (n - 1.0) * unit
        tiles = inverse_factor_rows([block[i : i + ROWS] for i in range(0, width, ROWS)], 4, 1)
        inverse = jnp.where(column <= row, jnp.concatenate(tiles, axis=0), 0.0)
        if end < n:
            near = precise_dot(work[end : end + width, begin:end], inverse, ((1,), (1,)))
            diagonal = work[end : end + width, end : end + width] - precise_dot(near, near, ((1,), (1,)))
            far = precise_dot(work[end + width :, begin:end], inverse, ((1,), (1,)))
            below = jnp.concatenate([near, far], axis=0)
        else:
            below = precise_dot(work[end:, begin:end], inverse, ((1,), (1,)))
        if begin > 0:
            work[begin:end, :begin] = precise_dot(inverse, work[begin:end, :begin])
            work[end:, :begin] = work[end:, :begin] - precise_dot(below, work[begin:end, :begin])
        work[begin:end, begin:end] = inverse
        work[end:, begin:end] = -precise_dot(below, inverse)
        if end + width < n:
            work[end + width :, end : end + width] = work[end + width :, end : end + width] - precise_dot(far, near, ((1,), (1,)))
            work[end + width :, end + width :] = work[end + width :, end + width :] - precise_dot(
                far, far[: n - end - width], ((1,), (1,))
            )
        elif end < n:
            work[n:, end:] = work[n:, end:] - precise_dot(far, near, ((1,), (1,)))
    shift = -work[n : n + 1, :]
    copies = []
    for begin in range(0, n, width):
        rows = slice(begin, begin + width)
        place = lax.broadcasted_iota(jnp.int32, (width, n), 0) + begin
        lower = lax.broadcasted_iota(jnp.int32, (width, n), 1) <= place
        mixing = (jnp.where(lower, work[rows, :] * math.sqrt(n - 1.0), 0.0) + shift).astype(jnp.bfloat16)
        out[rows, :] = mean_ref[...] + jnp.dot(mixing, anomaly_ref[...], preferred_element_type=F32)
        copies.append(pltpu.make_async_copy(out.at[rows], out_hbm.at[rows], sems.at[begin // width]))
        copies[-1].start()
    for copy in copies:
        copy.wait()


def analysis(packed, pull_tile, anomaly, mean):
    n, here = anomaly.shape
    return pl.pallas_call(
        functools.partial(analysis_kernel, n, LANES),
        out_shape=jax.ShapeDtypeStruct((n, here), F32),
        in_specs=[pl.BlockSpec(memory_space=pltpu.VMEM)] * 4,
        out_specs=pl.BlockSpec(memory_space=pltpu.HBM),
        scratch_shapes=[
            pltpu.VMEM((n + ROWS, n), F32),
            pltpu.VMEM((n, here), F32),
            pltpu.SemaphoreType.DMA((n // LANES,)),
        ],
        compiler_params=pltpu.CompilerParams(vmem_limit_bytes=24 << 20),
        name="analysis",
    )(packed, pull_tile, anomaly, mean)


def local(
    background_copies,
    measuring_span_leading_cell,
    measuring_kernel_coefficients,
    measured_readings,
    measured_error_precision,
):
    total, pulled, copy_anomalies, predicted_centroid = front(
        background_copies,
        measuring_span_leading_cell[None, :],
        jnp.transpose(measuring_kernel_coefficients),
        measured_readings[None, :],
        measured_error_precision[None, :],
        N_Y,
        lax.axis_size("cells") // N_Y,
    )
    return analysis(total, pulled, copy_anomalies, predicted_centroid)


def solution(mesh):
    in_specs = (
        P("mem", "cells"),
        P(("cells", "mem")),
        P(("cells", "mem"), None),
        P(("cells", "mem")),
        P(("cells", "mem")),
    )
    out_specs = P(None, ("cells", "mem"))
    return jax.shard_map(local, mesh=mesh, in_specs=in_specs, out_specs=out_specs, check_vma=False)
```

```python
import functools
import math

import jax
import jax.numpy as jnp
from jax import lax
from jax.experimental import pallas as pl
from jax.experimental.pallas import tpu as pltpu
from jax.sharding import PartitionSpec as P

F32 = jnp.float32
N_Y = 4
N_CORE = 2
ROWS, LANES = 8, 128
MESH = pl.DeviceIdType.MESH


def front_kernel(n_mem, n_y, n_z, field_ref, start_hbm, weight_hbm, reading_hbm, precision_hbm,
                 total_ref, pulled_ref, anomaly_ref, mean_ref,
                 start_ref, weight_ref, reading_ref, precision_ref, state, spread_out, table, weighted, a_local, a_core, b_local, b_core,
                 a_out, a_in, b_out, b_in, ay_out, ay_in, bx_out, bx_in, az, bz,
                 small_sem, own_sem, edge_send, edge_recv, x_send, x_recv,
                 core_sem, a_sem, b_sem, ay_sem, bx_sem, az_sem, bz_sem, ag_sem, bg_sem, ah_sem, bh_sem, pair_sem):
    cell, mem = lax.axis_index("cells"), lax.axis_index("mem")
    n_cells = n_y * n_z
    y, z = lax.rem(cell, n_y), cell // n_y
    n_x = n_mem // N_CORE
    x, core = mem // N_CORE, lax.rem(mem, N_CORE)
    members = field_ref.shape[0]
    n = members * n_mem
    here = anomaly_ref.shape[1]
    wide = state.shape[1]
    edge = wide - here
    last = n_mem - 1

    def mem_peer(step):
        return (cell, lax.rem(mem + step, n_mem))

    def x_peer(step):
        return (cell, lax.rem(x + step, n_x) * N_CORE + core)

    def core_peer(step):
        return (cell, x * N_CORE + lax.rem(core + step, N_CORE))

    def y_peer(step):
        return (z * n_y + lax.rem(y + step, n_y), mem)

    def z_peer(step):
        return (lax.rem(z + step, n_z) * n_y + y, mem)

    def signal(peer):
        pl.semaphore_signal(barrier, inc=1, device_id=peer, device_id_type=MESH)

    small = [
        pltpu.make_async_copy(source, target, small_sem.at[index])
        for index, (source, target) in enumerate(
            ((start_hbm, start_ref), (weight_hbm, weight_ref), (reading_hbm, reading_ref), (precision_hbm, precision_ref))
        )
    ]
    for copy in small:
        copy.start()

    barrier = pltpu.get_barrier_semaphore()
    for step in range(1, n_mem):
        signal(mem_peer(step))
    for step in range(1, n_y):
        signal(y_peer(step))
    for step in range(1, n_z):
        signal(z_peer(step))

    @pl.when(mem == last)
    def _():
        for source in range(n_mem):
            signal((lax.rem(cell + 1, n_cells), source))

    rows_here = pl.ds(pl.multiple_of(mem * members, members), members)

    def own_copy(width):
        return pltpu.make_async_copy(
            field_ref.at[:, pl.ds(pl.multiple_of(mem * here, here), width)],
            state.at[rows_here, pl.ds(0, width)], own_sem,
        )

    @pl.when(mem != last)
    def _():
        own_copy(wide).start()

    @pl.when(mem == last)
    def _():
        own_copy(here).start()

    pl.semaphore_wait(barrier, n_mem + n_y + n_z - 2)

    def slab_copy(step, width):
        target = lax.rem(mem + step, n_mem)
        return pltpu.make_async_remote_copy(
            src_ref=field_ref.at[:, pl.ds(pl.multiple_of(target * here, here), width)],
            dst_ref=state.at[rows_here, pl.ds(0, width)],
            send_sem=x_send.at[step - 1], recv_sem=x_recv.at[step - 1],
            device_id=mem_peer(step), device_id_type=MESH,
        )

    def arrival(step, width):
        source = lax.rem(mem + n_mem - step, n_mem)
        rows = pl.ds(pl.multiple_of(source * members, members), members)
        return pltpu.make_async_remote_copy(
            src_ref=field_ref.at[:, pl.ds(0, width)], dst_ref=state.at[rows, pl.ds(0, width)],
            send_sem=x_send.at[step - 1], recv_sem=x_recv.at[step - 1],
            device_id=mem_peer(step), device_id_type=MESH,
        )

    def edge_copy(source):
        rows = pl.ds(pl.multiple_of(source * members, members), members)
        return pltpu.make_async_remote_copy(
            src_ref=field_ref.at[:, pl.ds(0, edge)], dst_ref=state.at[rows, pl.ds(here, edge)],
            send_sem=edge_send, recv_sem=edge_recv.at[source],
            device_id=(lax.rem(cell + n_cells - 1, n_cells), last), device_id_type=MESH,
        )

    for step in range(1, n_mem):
        target = lax.rem(mem + step, n_mem)

        @pl.when(target != last)
        def _(step=step):
            slab_copy(step, wide).start()

        @pl.when(target == last)
        def _(step=step):
            slab_copy(step, here).start()

    edge_copy(mem).start()

    for copy in small:
        copy.wait()
    start = start_ref[...]
    taps = [weight_ref[j : j + 1, :].astype(F32) for j in range(weight_ref.shape[0])]
    chunk = 64

    @pl.loop(0, wide // chunk)
    def _(index):
        first = pl.multiple_of(index * chunk, chunk)
        ahead = lax.broadcasted_iota(jnp.int32, (chunk, start.shape[1]), 0) + first - start
        block = jnp.zeros(ahead.shape, F32)
        for j, tap in enumerate(taps):
            block = jnp.where(ahead == j, tap, block)
        table[pl.ds(first, chunk), :] = block.astype(jnp.bfloat16)

    @pl.when(mem != last)
    def _():
        own_copy(wide).wait()
        for step in range(1, n_mem):
            arrival(step, wide).wait_recv()

    @pl.when(mem == last)
    def _():
        own_copy(here).wait()
        for step in range(1, n_mem):
            arrival(step, here).wait_recv()
        for source in range(n_mem):
            edge_copy(source).wait_recv()

    step_rows = 64

    def add_rows(index, total):
        first = pl.multiple_of(index * step_rows, step_rows)
        return total + jnp.sum(state[pl.ds(first, step_rows), :].astype(F32).reshape(step_rows // ROWS, ROWS, wide), axis=0)

    sums = lax.fori_loop(0, n // step_rows, add_rows, jnp.zeros((ROWS, wide), F32))
    mean = jnp.sum(sums, axis=0, keepdims=True) / n
    mean_ref[...] = mean[:, :here]

    @pl.loop(0, n // step_rows)
    def _(index):
        rows = pl.ds(pl.multiple_of(index * step_rows, step_rows), step_rows)
        away = (state[rows, :].astype(F32) - mean).astype(jnp.bfloat16)
        spread_out[rows, :] = away
        anomaly_ref[rows, :] = away[:, :here]

    high = mean.astype(jnp.bfloat16)
    rest = mean - high.astype(F32)
    middle = rest.astype(jnp.bfloat16)
    small = (rest - middle.astype(F32)).astype(jnp.bfloat16)
    spread_out[n:, :] = jnp.concatenate([high, middle, small, jnp.zeros((13, wide), jnp.bfloat16)], axis=0)
    projected = jnp.dot(spread_out[...], table[...], preferred_element_type=F32)
    root = jnp.sqrt(precision_ref[...])
    observed = projected[n : n + 1] + (projected[n + 1 : n + 2] + projected[n + 2 : n + 3])
    innovation = (root * (reading_ref[...] - observed)).astype(jnp.bfloat16)
    weighted[:n, :] = (root * projected[:n]).astype(jnp.bfloat16)
    weighted[n:, :] = jnp.concatenate([innovation, jnp.zeros((15, innovation.shape[1]), jnp.bfloat16)], axis=0)

    a_piece = a_out.shape[1] - ROWS
    b_piece = b_out.shape[1]
    a_rows, b_rows = n_x * a_piece, n_y * b_piece
    half = a_rows + b_rows
    place = 0
    pull = []
    for begin in range(0, n, LANES):
        product = lax.dot_general(
            weighted[begin:, :], weighted[begin : begin + LANES, :], (((1,), (1,)), ((), ())), preferred_element_type=F32
        )
        pull.append(product[n - begin : n - begin + 1])
        for row in range(0, n - begin, ROWS):
            tile = product[row : row + ROWS]
            side, spot = place // half, place % half
            if spot < a_rows:
                a_local[side, spot // a_piece, spot % a_piece : spot % a_piece + ROWS, :] = tile
            else:
                spot -= a_rows
                b_local[side, spot // b_piece, spot % b_piece : spot % b_piece + ROWS, :] = tile
            place += ROWS
    pull_tile = jnp.concatenate(pull + [jnp.zeros((ROWS - len(pull), LANES), F32)], axis=0)
    for side in range(N_CORE):
        for s in range(n_x):
            a_local[side, s, a_piece:, :] = pull_tile

    def begin_all(sources, target, peer, sems, count):
        copies = [
            pltpu.make_async_remote_copy(
                src_ref=sources(step), dst_ref=target(step), send_sem=sems.at[0, step - 1], recv_sem=sems.at[1, step - 1],
                device_id=peer(step), device_id_type=MESH,
            )
            for step in range(1, count)
        ]
        for copy in copies:
            copy.start()
        pending.extend(copies)
        return copies

    def arrived(copies):
        for copy in copies:
            copy.wait_recv()

    pending = []
    a_part = az.shape[1] - ROWS
    b_part = bz.shape[1]
    other = lax.rem(core + 1, N_CORE)
    a0 = begin_all(lambda s: a_local.at[other], lambda s: a_core, core_peer, core_sem.at[0], N_CORE)
    b0 = begin_all(lambda s: b_local.at[other], lambda s: b_core, core_peer, core_sem.at[1], N_CORE)
    arrived(a0)
    a_out[...] = a_local[core] + a_core[...]
    a1 = begin_all(lambda s: a_out.at[lax.rem(x + s, n_x)], lambda s: a_in.at[s - 1], x_peer, a_sem, n_x)
    arrived(b0)
    b_out[...] = b_local[core] + b_core[...]
    b1 = begin_all(lambda s: b_out.at[lax.rem(y + s, n_y)], lambda s: b_in.at[s - 1], y_peer, b_sem, n_y)
    arrived(a1)
    summed = a_out[x]
    for s in range(n_x - 1):
        summed = summed + a_in[s]
    for s in range(n_y):
        ay_out[s, :a_part, :] = summed[s * a_part : (s + 1) * a_part]
        ay_out[s, a_part:, :] = summed[a_piece:]
    a2 = begin_all(lambda s: ay_out.at[lax.rem(y + s, n_y)], lambda s: ay_in.at[s - 1], y_peer, ay_sem, n_y)
    arrived(b1)
    summed = b_out[y]
    for s in range(n_y - 1):
        summed = summed + b_in[s]
    for s in range(n_x):
        bx_out[s] = summed[s * b_part : (s + 1) * b_part]
    b2 = begin_all(lambda s: bx_out.at[lax.rem(x + s, n_x)], lambda s: bx_in.at[s - 1], x_peer, bx_sem, n_x)
    arrived(a2)
    summed = ay_out[y]
    for s in range(n_y - 1):
        summed = summed + ay_in[s]
    az[z] = summed
    a3 = begin_all(lambda s: az.at[z], lambda s: az.at[z], z_peer, az_sem, n_z)
    arrived(b2)
    summed = bx_out[x]
    for s in range(n_x - 1):
        summed = summed + bx_in[s]
    bz[z] = summed
    b3 = begin_all(lambda s: bz.at[z], lambda s: bz.at[z], z_peer, bz_sem, n_z)
    arrived(a3)
    summed = az[0]
    for s in range(1, n_z):
        summed = summed + az[s]
    pulled_ref[...] = summed[a_part:]
    base = core * half
    a_slab = pl.ds(pl.multiple_of(base + x * a_piece, ROWS), a_piece)
    a_own = pl.ds(pl.multiple_of(base + x * a_piece + y * a_part, ROWS), a_part)
    total_ref[a_own, :] = summed[:a_part]
    a4 = begin_all(lambda s: total_ref.at[a_own], lambda s: total_ref.at[a_own], y_peer, ag_sem, n_y)
    arrived(b3)
    summed = bz[0]
    for s in range(1, n_z):
        summed = summed + bz[s]
    b_slab = pl.ds(pl.multiple_of(base + a_rows + y * b_piece, ROWS), b_piece)
    b_own = pl.ds(pl.multiple_of(base + a_rows + y * b_piece + x * b_part, ROWS), b_part)
    total_ref[b_own, :] = summed
    b4 = begin_all(lambda s: total_ref.at[b_own], lambda s: total_ref.at[b_own], x_peer, bg_sem, n_x)
    arrived(a4)
    a5 = begin_all(lambda s: total_ref.at[a_slab], lambda s: total_ref.at[a_slab], x_peer, ah_sem, n_x)
    arrived(b4)
    b5 = begin_all(lambda s: total_ref.at[b_slab], lambda s: total_ref.at[b_slab], y_peer, bh_sem, n_y)
    a_all = pl.ds(pl.multiple_of(base, ROWS), a_rows)
    b_all = pl.ds(pl.multiple_of(base + a_rows, ROWS), b_rows)
    arrived(a5)
    a6 = begin_all(lambda s: total_ref.at[a_all], lambda s: total_ref.at[a_all], core_peer, pair_sem.at[0], N_CORE)
    arrived(b5)
    b6 = begin_all(lambda s: total_ref.at[b_all], lambda s: total_ref.at[b_all], core_peer, pair_sem.at[1], N_CORE)
    arrived(a6)
    arrived(b6)
    for copy in pending:
        copy.wait_send()
    edge_copy(mem).wait_send()
    for step in range(1, n_mem):
        target = lax.rem(mem + step, n_mem)

        @pl.when(target != last)
        def _(step=step):
            slab_copy(step, wide).wait_send()

        @pl.when(target == last)
        def _(step=step):
            slab_copy(step, here).wait_send()


def front(field, start, weights, readings, precision, n_y, n_z):
    members, slab = field.shape
    n_mem = lax.axis_size("mem")
    n, here = members * n_mem, slab // n_mem
    observations = start.shape[1]
    blocks = n // LANES
    packed = LANES * blocks * (blocks + 1) // 2
    n_x = n_mem // N_CORE
    a_part = packed * 3 // 5 // (n_mem * n_y)
    b_part = (packed - a_part * n_mem * n_y) // (n_mem * n_y)
    a_piece, b_piece = a_part * n_y, b_part * n_x
    dma = pltpu.SemaphoreType.DMA
    vmem = pl.BlockSpec(memory_space=pltpu.VMEM)
    bf16 = jnp.bfloat16
    return pl.pallas_call(
        functools.partial(front_kernel, n_mem, n_y, n_z),
        out_shape=(
            jax.ShapeDtypeStruct((packed, LANES), F32),
            jax.ShapeDtypeStruct((ROWS, LANES), F32),
            jax.ShapeDtypeStruct((n, here), bf16),
            jax.ShapeDtypeStruct((1, here), F32),
        ),
        in_specs=[pl.BlockSpec(memory_space=pltpu.HBM)] * 5,
        out_specs=(vmem,) * 4,
        scratch_shapes=[
            pltpu.VMEM(start.shape, start.dtype),
            pltpu.VMEM(weights.shape, weights.dtype),
            pltpu.VMEM(readings.shape, readings.dtype),
            pltpu.VMEM(precision.shape, precision.dtype),
            pltpu.VMEM((n, here + LANES), bf16),
            pltpu.VMEM((n + 16, here + LANES), bf16),
            pltpu.VMEM((here + LANES, observations), bf16),
            pltpu.VMEM((n + 16, observations), bf16),
            pltpu.VMEM((N_CORE, n_x, a_piece + ROWS, LANES), F32),
            pltpu.VMEM((n_x, a_piece + ROWS, LANES), F32),
            pltpu.VMEM((N_CORE, n_y, b_piece, LANES), F32),
            pltpu.VMEM((n_y, b_piece, LANES), F32),
            pltpu.VMEM((n_x, a_piece + ROWS, LANES), F32),
            pltpu.VMEM((n_x - 1, a_piece + ROWS, LANES), F32),
            pltpu.VMEM((n_y, b_piece, LANES), F32),
            pltpu.VMEM((n_y - 1, b_piece, LANES), F32),
            pltpu.VMEM((n_y, a_part + ROWS, LANES), F32),
            pltpu.VMEM((n_y - 1, a_part + ROWS, LANES), F32),
            pltpu.VMEM((n_x, b_part, LANES), F32),
            pltpu.VMEM((n_x - 1, b_part, LANES), F32),
            pltpu.VMEM((n_z, a_part + ROWS, LANES), F32),
            pltpu.VMEM((n_z, b_part, LANES), F32),
            dma((4,)), dma, dma, dma((n_mem,)), dma((n_mem - 1,)), dma((n_mem - 1,)),
            dma((2, 2, N_CORE - 1)),
            dma((2, n_x - 1)), dma((2, n_y - 1)), dma((2, n_y - 1)), dma((2, n_x - 1)),
            dma((2, n_z - 1)), dma((2, n_z - 1)),
            dma((2, n_y - 1)), dma((2, n_x - 1)), dma((2, n_x - 1)), dma((2, n_y - 1)),
            dma((2, 2, N_CORE - 1)),
        ],
        compiler_params=pltpu.CompilerParams(collective_id=0, has_side_effects=True, vmem_limit_bytes=20 << 20),
        name="front",
    )(*(pltpu.with_memory_space_constraint(x, pltpu.HBM) for x in (field, start, weights, readings, precision)))

def precise_dot(left, right, contract=((1,), (0,))):
    return lax.dot_general(
        left, right, (contract, ((), ())), precision=lax.Precision.HIGHEST, preferred_element_type=F32
    )


def inverse_factor_rows(tiles, panel, ahead):
    tiles = list(tiles)
    count = len(tiles)
    extent = tiles[0].shape[1]
    lane = lax.broadcasted_iota(jnp.int32, (ROWS, extent), 1)
    sublane = lax.broadcasted_iota(jnp.int32, (ROWS, extent), 0)

    def spread(value):
        return jnp.broadcast_to(value, (ROWS, extent))

    def pick(tile, position):
        return jnp.take_along_axis(tile, jnp.full((ROWS, extent), position, jnp.int32), axis=1)

    for home in range(count):
        first = home * ROWS
        panel_end = min((home // panel + 1) * panel, count)
        near_end = max(min(panel_end + ahead, count), min(home + 2, count))
        own = tiles[home]
        lanes = later if home else [pick(own, first + a) for a in range(ROWS)]
        pivots = {(b, a): spread(lanes[a][b : b + 1, :]) for a in range(ROWS) for b in range(a, ROWS)}
        member = (lane >= first) & (lane < first + ROWS)
        rows = [
            jnp.where(member, jnp.where(lane == first + a, 1.0, 0.0), spread(own[a : a + 1, :])) for a in range(ROWS)
        ]
        scales = []
        following = tiles[home + 1] if home + 1 < count else None
        if following is not None:
            columns = [pick(following, first + a) for a in range(ROWS)]
            later = [pick(following, first + ROWS + c) for c in range(ROWS)]
            following = jnp.where(member, 0.0, following)
        for a in range(ROWS):
            scale = lax.rsqrt(pivots[(a, a)])
            scales.append(scale)
            rows[a] = rows[a] * scale
            for b in range(a + 1, ROWS):
                pivots[(b, a)] = pivots[(b, a)] * scale
            for b in range(a + 1, ROWS):
                for c in range(a + 1, b + 1):
                    pivots[(b, c)] = pivots[(b, c)] - pivots[(b, a)] * pivots[(c, a)]
                rows[b] = rows[b] - pivots[(b, a)] * rows[a]
            if following is not None:
                columns[a] = columns[a] * scale
                for b in range(a + 1, ROWS):
                    columns[b] = columns[b] - columns[a] * pivots[(b, a)]
                following = following - columns[a] * rows[a]
                later = [part - columns[a] * spread(columns[a][c : c + 1, :]) for c, part in enumerate(later)]
        fresh = rows[0]
        for a in range(1, ROWS):
            fresh = jnp.where(sublane == a, rows[a], fresh)
        tiles[home] = fresh
        solved = list(rows)
        for a in range(ROWS - 1, -1, -1):
            solved[a] = solved[a] * scales[a]
            for b in range(a):
                solved[b] = solved[b] - pivots[(a, b)] * solved[a]
        if following is not None:
            tiles[home + 1] = following
        for index in range(home + 2, near_end):
            tile = tiles[index]
            fresh = jnp.where(member, 0.0, tile)
            for a in range(ROWS):
                fresh = fresh - pick(tile, first + a) * solved[a]
            tiles[index] = fresh
        if home + 1 == panel_end and near_end < count:
            begin = (home // panel) * panel
            done = tiles[begin:panel_end]
            masked = [
                jnp.where((lane >= (begin + i + 1) * ROWS) & (lane < panel_end * ROWS), 0.0, tile)
                for i, tile in enumerate(done)
            ]
            change = precise_dot(jnp.concatenate(done, axis=0), jnp.concatenate(masked, axis=0), ((0,), (0,)))
            inside = (lane >= begin * ROWS) & (lane < panel_end * ROWS)
            for index in range(near_end, count):
                tiles[index] = jnp.where(inside, 0.0, tiles[index]) - change[index * ROWS : (index + 1) * ROWS]
    return tiles


def analysis_kernel(n, width, packed_ref, pull_ref, anomaly_ref, mean_ref, out_hbm, work, out, sems):
    shape = (width, width)
    row = lax.broadcasted_iota(jnp.int32, shape, 0)
    column = lax.broadcasted_iota(jnp.int32, shape, 1)
    unit = jnp.where(row == column, 1.0, 0.0)
    place = 0
    for begin in range(0, n, width):
        work[begin:n, begin : begin + width] = packed_ref[place : place + n - begin, :]
        place += n - begin
        index = begin // width
        work[n : n + 1, begin : begin + width] = pull_ref[index : index + 1, :]
    work[n + 1 :, :] = jnp.zeros((ROWS - 1, n), F32)
    diagonal = work[:width, :width]
    for begin in range(0, n, width):
        end = begin + width
        block = diagonal + (n - 1.0) * unit
        tiles = inverse_factor_rows([block[i : i + ROWS] for i in range(0, width, ROWS)], 4, 1)
        inverse = jnp.where(column <= row, jnp.concatenate(tiles, axis=0), 0.0)
        if end < n:
            near = precise_dot(work[end : end + width, begin:end], inverse, ((1,), (1,)))
            diagonal = work[end : end + width, end : end + width] - precise_dot(near, near, ((1,), (1,)))
            far = precise_dot(work[end + width :, begin:end], inverse, ((1,), (1,)))
            below = jnp.concatenate([near, far], axis=0)
        else:
            below = precise_dot(work[end:, begin:end], inverse, ((1,), (1,)))
        if begin > 0:
            work[begin:end, :begin] = precise_dot(inverse, work[begin:end, :begin])
            work[end:, :begin] = work[end:, :begin] - precise_dot(below, work[begin:end, :begin])
        work[begin:end, begin:end] = inverse
        work[end:, begin:end] = -precise_dot(below, inverse)
        if end + width < n:
            work[end + width :, end : end + width] = work[end + width :, end : end + width] - precise_dot(far, near, ((1,), (1,)))
            work[end + width :, end + width :] = work[end + width :, end + width :] - precise_dot(
                far, far[: n - end - width], ((1,), (1,))
            )
        elif end < n:
            work[n:, end:] = work[n:, end:] - precise_dot(far, near, ((1,), (1,)))
    shift = -work[n : n + 1, :]
    copies = []
    for begin in range(0, n, width):
        rows = slice(begin, begin + width)
        place = lax.broadcasted_iota(jnp.int32, (width, n), 0) + begin
        lower = lax.broadcasted_iota(jnp.int32, (width, n), 1) <= place
        mixing = (jnp.where(lower, work[rows, :] * math.sqrt(n - 1.0), 0.0) + shift).astype(jnp.bfloat16)
        out[rows, :] = mean_ref[...] + jnp.dot(mixing, anomaly_ref[...], preferred_element_type=F32)
        copies.append(pltpu.make_async_copy(out.at[rows], out_hbm.at[rows], sems.at[begin // width]))
        copies[-1].start()
    for copy in copies:
        copy.wait()


def analysis(packed, pull_tile, anomaly, mean):
    n, here = anomaly.shape
    return pl.pallas_call(
        functools.partial(analysis_kernel, n, LANES),
        out_shape=jax.ShapeDtypeStruct((n, here), F32),
        in_specs=[pl.BlockSpec(memory_space=pltpu.VMEM)] * 4,
        out_specs=pl.BlockSpec(memory_space=pltpu.HBM),
        scratch_shapes=[
            pltpu.VMEM((n + ROWS, n), F32),
            pltpu.VMEM((n, here), F32),
            pltpu.SemaphoreType.DMA((n // LANES,)),
        ],
        compiler_params=pltpu.CompilerParams(vmem_limit_bytes=24 << 20),
        name="analysis",
    )(packed, pull_tile, anomaly, mean)


def local(
    background_copies,
    measuring_span_leading_cell,
    measuring_kernel_coefficients,
    measured_readings,
    measured_error_precision,
):
    total, pulled, copy_anomalies, predicted_centroid = front(
        background_copies,
        measuring_span_leading_cell[None, :],
        jnp.transpose(measuring_kernel_coefficients),
        measured_readings[None, :],
        measured_error_precision[None, :],
        N_Y,
        lax.axis_size("cells") // N_Y,
    )
    return analysis(total, pulled, copy_anomalies, predicted_centroid)


def solution(mesh):
    in_specs = (
        P("mem", "cells"),
        P(("cells", "mem")),
        P(("cells", "mem"), None),
        P(("cells", "mem")),
        P(("cells", "mem")),
    )
    out_specs = P(None, ("cells", "mem"))
    return jax.shard_map(local, mesh=mesh, in_specs=in_specs, out_specs=out_specs, check_vma=False)
```

```python
import functools
import math

import jax
import jax.numpy as jnp
from jax import lax
from jax.experimental import pallas as pl
from jax.experimental.pallas import tpu as pltpu
from jax.sharding import PartitionSpec as P

F32 = jnp.float32
N_Y = 4
N_CORE = 2
ROWS, LANES = 8, 128
MESH = pl.DeviceIdType.MESH


def front_kernel(n_mem, n_y, n_z, field_ref, start_hbm, weight_hbm, reading_hbm, precision_hbm,
                 total_ref, pulled_ref, anomaly_ref, mean_ref,
                 start_ref, weight_ref, reading_ref, precision_ref, state, spread_out, table, weighted, local_sums, core_in, plane_out, plane_in, z_in,
                 small_sem, own_sem, edge_send, edge_recv, x_send, x_recv,
                 core_sem, plane_sem, z_sem, gather_sem, pair_sem):
    cell, mem = lax.axis_index("cells"), lax.axis_index("mem")
    n_cells = n_y * n_z
    y, z = lax.rem(cell, n_y), cell // n_y
    n_x = n_mem // N_CORE
    x, core = mem // N_CORE, lax.rem(mem, N_CORE)
    members = field_ref.shape[0]
    n = members * n_mem
    here = anomaly_ref.shape[1]
    wide = state.shape[1]
    edge = wide - here
    last = n_mem - 1

    def mem_peer(step):
        return (cell, lax.rem(mem + step, n_mem))

    n_plane = n_x * n_y
    spot_here = x * n_y + y

    def plane_peer(step):
        spot = lax.rem(spot_here + step, n_plane)
        return (z * n_y + lax.rem(spot, n_y), (spot // n_y) * N_CORE + core)

    def core_peer(step):
        return (cell, x * N_CORE + lax.rem(core + step, N_CORE))

    def z_peer(step):
        return (lax.rem(z + step, n_z) * n_y + y, mem)

    def signal(peer):
        pl.semaphore_signal(barrier, inc=1, device_id=peer, device_id_type=MESH)

    small = [
        pltpu.make_async_copy(source, target, small_sem.at[index])
        for index, (source, target) in enumerate(
            ((start_hbm, start_ref), (weight_hbm, weight_ref), (reading_hbm, reading_ref), (precision_hbm, precision_ref))
        )
    ]
    for copy in small:
        copy.start()

    barrier = pltpu.get_barrier_semaphore()
    for step in range(1, n_mem):
        signal(mem_peer(step))
    for step in range(1, n_plane):
        signal(plane_peer(step))
    for step in range(1, n_z):
        signal(z_peer(step))

    @pl.when(mem == last)
    def _():
        for source in range(n_mem):
            signal((lax.rem(cell + 1, n_cells), source))

    rows_here = pl.ds(pl.multiple_of(mem * members, members), members)

    def own_copy(width):
        return pltpu.make_async_copy(
            field_ref.at[:, pl.ds(pl.multiple_of(mem * here, here), width)],
            state.at[rows_here, pl.ds(0, width)], own_sem,
        )

    @pl.when(mem != last)
    def _():
        own_copy(wide).start()

    @pl.when(mem == last)
    def _():
        own_copy(here).start()

    pl.semaphore_wait(barrier, n_mem + n_plane + n_z - 2)

    def slab_copy(step, width):
        target = lax.rem(mem + step, n_mem)
        return pltpu.make_async_remote_copy(
            src_ref=field_ref.at[:, pl.ds(pl.multiple_of(target * here, here), width)],
            dst_ref=state.at[rows_here, pl.ds(0, width)],
            send_sem=x_send.at[step - 1], recv_sem=x_recv.at[step - 1],
            device_id=mem_peer(step), device_id_type=MESH,
        )

    def arrival(step, width):
        source = lax.rem(mem + n_mem - step, n_mem)
        rows = pl.ds(pl.multiple_of(source * members, members), members)
        return pltpu.make_async_remote_copy(
            src_ref=field_ref.at[:, pl.ds(0, width)], dst_ref=state.at[rows, pl.ds(0, width)],
            send_sem=x_send.at[step - 1], recv_sem=x_recv.at[step - 1],
            device_id=mem_peer(step), device_id_type=MESH,
        )

    def edge_copy(source):
        rows = pl.ds(pl.multiple_of(source * members, members), members)
        return pltpu.make_async_remote_copy(
            src_ref=field_ref.at[:, pl.ds(0, edge)], dst_ref=state.at[rows, pl.ds(here, edge)],
            send_sem=edge_send, recv_sem=edge_recv.at[source],
            device_id=(lax.rem(cell + n_cells - 1, n_cells), last), device_id_type=MESH,
        )

    for step in range(1, n_mem):
        target = lax.rem(mem + step, n_mem)

        @pl.when(target != last)
        def _(step=step):
            slab_copy(step, wide).start()

        @pl.when(target == last)
        def _(step=step):
            slab_copy(step, here).start()

    edge_copy(mem).start()

    for copy in small:
        copy.wait()
    start = start_ref[...]
    taps = [weight_ref[j : j + 1, :].astype(F32) for j in range(weight_ref.shape[0])]
    chunk = 64

    @pl.loop(0, wide // chunk)
    def _(index):
        first = pl.multiple_of(index * chunk, chunk)
        ahead = lax.broadcasted_iota(jnp.int32, (chunk, start.shape[1]), 0) + first - start
        block = jnp.zeros(ahead.shape, F32)
        for j, tap in enumerate(taps):
            block = jnp.where(ahead == j, tap, block)
        table[pl.ds(first, chunk), :] = block.astype(jnp.bfloat16)

    @pl.when(mem != last)
    def _():
        own_copy(wide).wait()
        for step in range(1, n_mem):
            arrival(step, wide).wait_recv()

    @pl.when(mem == last)
    def _():
        own_copy(here).wait()
        for step in range(1, n_mem):
            arrival(step, here).wait_recv()
        for source in range(n_mem):
            edge_copy(source).wait_recv()

    step_rows = 64

    def add_rows(index, total):
        first = pl.multiple_of(index * step_rows, step_rows)
        return total + jnp.sum(state[pl.ds(first, step_rows), :].astype(F32).reshape(step_rows // ROWS, ROWS, wide), axis=0)

    sums = lax.fori_loop(0, n // step_rows, add_rows, jnp.zeros((ROWS, wide), F32))
    mean = jnp.sum(sums, axis=0, keepdims=True) / n
    mean_ref[...] = mean[:, :here]

    @pl.loop(0, n // step_rows)
    def _(index):
        rows = pl.ds(pl.multiple_of(index * step_rows, step_rows), step_rows)
        away = (state[rows, :].astype(F32) - mean).astype(jnp.bfloat16)
        spread_out[rows, :] = away
        anomaly_ref[rows, :] = away[:, :here]

    high = mean.astype(jnp.bfloat16)
    rest = mean - high.astype(F32)
    middle = rest.astype(jnp.bfloat16)
    small = (rest - middle.astype(F32)).astype(jnp.bfloat16)
    spread_out[n:, :] = jnp.concatenate([high, middle, small, jnp.zeros((13, wide), jnp.bfloat16)], axis=0)
    projected = jnp.dot(spread_out[...], table[...], preferred_element_type=F32)
    root = jnp.sqrt(precision_ref[...])
    observed = projected[n : n + 1] + (projected[n + 1 : n + 2] + projected[n + 2 : n + 3])
    innovation = (root * (reading_ref[...] - observed)).astype(jnp.bfloat16)
    weighted[:n, :] = (root * projected[:n]).astype(jnp.bfloat16)
    weighted[n:, :] = jnp.concatenate([innovation, jnp.zeros((15, innovation.shape[1]), jnp.bfloat16)], axis=0)

    part = plane_out.shape[1] - ROWS
    half = n_plane * part
    place = 0
    pull = []
    for begin in range(0, n, LANES):
        product = lax.dot_general(
            weighted[begin:, :], weighted[begin : begin + LANES, :], (((1,), (1,)), ((), ())), preferred_element_type=F32
        )
        pull.append(product[n - begin : n - begin + 1])
        for row in range(0, n - begin, ROWS):
            side, spot = place // half, place % half
            local_sums[side, spot // part, spot % part : spot % part + ROWS, :] = product[row : row + ROWS]
            place += ROWS
    pull_tile = jnp.concatenate(pull + [jnp.zeros((ROWS - len(pull), LANES), F32)], axis=0)
    for side in range(N_CORE):
        for s in range(n_plane):
            local_sums[side, s, part:, :] = pull_tile

    def begin_all(sources, target, peer, sems, count):
        copies = [
            pltpu.make_async_remote_copy(
                src_ref=sources(step), dst_ref=target(step), send_sem=sems.at[0, step - 1], recv_sem=sems.at[1, step - 1],
                device_id=peer(step), device_id_type=MESH,
            )
            for step in range(1, count)
        ]
        for copy in copies:
            copy.start()
        pending.extend(copies)
        return copies

    def arrived(copies):
        for copy in copies:
            copy.wait_recv()

    pending = []
    other = lax.rem(core + 1, N_CORE)
    arrived(begin_all(lambda s: local_sums.at[other], lambda s: core_in, core_peer, core_sem, N_CORE))
    plane_out[...] = local_sums[core] + core_in[...]
    arrived(
        begin_all(
            lambda s: plane_out.at[lax.rem(spot_here + s, n_plane)], lambda s: plane_in.at[s - 1], plane_peer, plane_sem, n_plane
        )
    )
    summed = plane_out[spot_here]
    for s in range(n_plane - 1):
        summed = summed + plane_in[s]
    z_in[z] = summed
    arrived(begin_all(lambda s: z_in.at[z], lambda s: z_in.at[z], z_peer, z_sem, n_z))
    summed = z_in[0]
    for s in range(1, n_z):
        summed = summed + z_in[s]
    pulled_ref[...] = summed[part:]
    base = core * half
    own = pl.ds(pl.multiple_of(base + spot_here * part, ROWS), part)
    total_ref[own, :] = summed[:part]
    arrived(begin_all(lambda s: total_ref.at[own], lambda s: total_ref.at[own], plane_peer, gather_sem, n_plane))
    mine = pl.ds(pl.multiple_of(base, ROWS), half)
    arrived(begin_all(lambda s: total_ref.at[mine], lambda s: total_ref.at[mine], core_peer, pair_sem, N_CORE))
    for copy in pending:
        copy.wait_send()
    edge_copy(mem).wait_send()
    for step in range(1, n_mem):
        target = lax.rem(mem + step, n_mem)

        @pl.when(target != last)
        def _(step=step):
            slab_copy(step, wide).wait_send()

        @pl.when(target == last)
        def _(step=step):
            slab_copy(step, here).wait_send()


def front(field, start, weights, readings, precision, n_y, n_z):
    members, slab = field.shape
    n_mem = lax.axis_size("mem")
    n, here = members * n_mem, slab // n_mem
    observations = start.shape[1]
    blocks = n // LANES
    packed = LANES * blocks * (blocks + 1) // 2
    n_plane = n_mem // N_CORE * n_y
    part = packed // (N_CORE * n_plane)
    dma = pltpu.SemaphoreType.DMA
    vmem = pl.BlockSpec(memory_space=pltpu.VMEM)
    bf16 = jnp.bfloat16
    return pl.pallas_call(
        functools.partial(front_kernel, n_mem, n_y, n_z),
        out_shape=(
            jax.ShapeDtypeStruct((packed, LANES), F32),
            jax.ShapeDtypeStruct((ROWS, LANES), F32),
            jax.ShapeDtypeStruct((n, here), bf16),
            jax.ShapeDtypeStruct((1, here), F32),
        ),
        in_specs=[pl.BlockSpec(memory_space=pltpu.HBM)] * 5,
        out_specs=(vmem,) * 4,
        scratch_shapes=[
            pltpu.VMEM(start.shape, start.dtype),
            pltpu.VMEM(weights.shape, weights.dtype),
            pltpu.VMEM(readings.shape, readings.dtype),
            pltpu.VMEM(precision.shape, precision.dtype),
            pltpu.VMEM((n, here + LANES), bf16),
            pltpu.VMEM((n + 16, here + LANES), bf16),
            pltpu.VMEM((here + LANES, observations), bf16),
            pltpu.VMEM((n + 16, observations), bf16),
            pltpu.VMEM((N_CORE, n_plane, part + ROWS, LANES), F32),
            pltpu.VMEM((n_plane, part + ROWS, LANES), F32),
            pltpu.VMEM((n_plane, part + ROWS, LANES), F32),
            pltpu.VMEM((n_plane - 1, part + ROWS, LANES), F32),
            pltpu.VMEM((n_z, part + ROWS, LANES), F32),
            dma((4,)), dma, dma, dma((n_mem,)), dma((n_mem - 1,)), dma((n_mem - 1,)),
            dma((2, N_CORE - 1)), dma((2, n_plane - 1)), dma((2, n_z - 1)), dma((2, n_plane - 1)), dma((2, N_CORE - 1)),
        ],
        compiler_params=pltpu.CompilerParams(collective_id=0, has_side_effects=True, vmem_limit_bytes=20 << 20),
        name="front",
    )(*(pltpu.with_memory_space_constraint(x, pltpu.HBM) for x in (field, start, weights, readings, precision)))

def precise_dot(left, right, contract=((1,), (0,))):
    return lax.dot_general(
        left, right, (contract, ((), ())), precision=lax.Precision.HIGHEST, preferred_element_type=F32
    )


def inverse_factor_rows(tiles, panel, ahead):
    tiles = list(tiles)
    count = len(tiles)
    extent = tiles[0].shape[1]
    lane = lax.broadcasted_iota(jnp.int32, (ROWS, extent), 1)
    sublane = lax.broadcasted_iota(jnp.int32, (ROWS, extent), 0)

    def spread(value):
        return jnp.broadcast_to(value, (ROWS, extent))

    def pick(tile, position):
        return jnp.take_along_axis(tile, jnp.full((ROWS, extent), position, jnp.int32), axis=1)

    for home in range(count):
        first = home * ROWS
        panel_end = min((home // panel + 1) * panel, count)
        near_end = max(min(panel_end + ahead, count), min(home + 2, count))
        own = tiles[home]
        lanes = later if home else [pick(own, first + a) for a in range(ROWS)]
        pivots = {(b, a): spread(lanes[a][b : b + 1, :]) for a in range(ROWS) for b in range(a, ROWS)}
        member = (lane >= first) & (lane < first + ROWS)
        rows = [
            jnp.where(member, jnp.where(lane == first + a, 1.0, 0.0), spread(own[a : a + 1, :])) for a in range(ROWS)
        ]
        scales = []
        following = tiles[home + 1] if home + 1 < count else None
        if following is not None:
            columns = [pick(following, first + a) for a in range(ROWS)]
            later = [pick(following, first + ROWS + c) for c in range(ROWS)]
            following = jnp.where(member, 0.0, following)
        for a in range(ROWS):
            scale = lax.rsqrt(pivots[(a, a)])
            scales.append(scale)
            rows[a] = rows[a] * scale
            for b in range(a + 1, ROWS):
                pivots[(b, a)] = pivots[(b, a)] * scale
            for b in range(a + 1, ROWS):
                for c in range(a + 1, b + 1):
                    pivots[(b, c)] = pivots[(b, c)] - pivots[(b, a)] * pivots[(c, a)]
                rows[b] = rows[b] - pivots[(b, a)] * rows[a]
            if following is not None:
                columns[a] = columns[a] * scale
                for b in range(a + 1, ROWS):
                    columns[b] = columns[b] - columns[a] * pivots[(b, a)]
                following = following - columns[a] * rows[a]
                later = [part - columns[a] * spread(columns[a][c : c + 1, :]) for c, part in enumerate(later)]
        fresh = rows[0]
        for a in range(1, ROWS):
            fresh = jnp.where(sublane == a, rows[a], fresh)
        tiles[home] = fresh
        solved = list(rows)
        for a in range(ROWS - 1, -1, -1):
            solved[a] = solved[a] * scales[a]
            for b in range(a):
                solved[b] = solved[b] - pivots[(a, b)] * solved[a]
        if following is not None:
            tiles[home + 1] = following
        for index in range(home + 2, near_end):
            tile = tiles[index]
            fresh = jnp.where(member, 0.0, tile)
            for a in range(ROWS):
                fresh = fresh - pick(tile, first + a) * solved[a]
            tiles[index] = fresh
        if home + 1 == panel_end and near_end < count:
            begin = (home // panel) * panel
            done = tiles[begin:panel_end]
            masked = [
                jnp.where((lane >= (begin + i + 1) * ROWS) & (lane < panel_end * ROWS), 0.0, tile)
                for i, tile in enumerate(done)
            ]
            change = precise_dot(jnp.concatenate(done, axis=0), jnp.concatenate(masked, axis=0), ((0,), (0,)))
            inside = (lane >= begin * ROWS) & (lane < panel_end * ROWS)
            for index in range(near_end, count):
                tiles[index] = jnp.where(inside, 0.0, tiles[index]) - change[index * ROWS : (index + 1) * ROWS]
    return tiles


def analysis_kernel(n, width, packed_ref, pull_ref, anomaly_ref, mean_ref, out_hbm, work, out, sems):
    shape = (width, width)
    row = lax.broadcasted_iota(jnp.int32, shape, 0)
    column = lax.broadcasted_iota(jnp.int32, shape, 1)
    unit = jnp.where(row == column, 1.0, 0.0)
    place = 0
    for begin in range(0, n, width):
        work[begin:n, begin : begin + width] = packed_ref[place : place + n - begin, :]
        place += n - begin
        index = begin // width
        work[n : n + 1, begin : begin + width] = pull_ref[index : index + 1, :]
    work[n + 1 :, :] = jnp.zeros((ROWS - 1, n), F32)
    diagonal = work[:width, :width]
    for begin in range(0, n, width):
        end = begin + width
        block = diagonal + (n - 1.0) * unit
        tiles = inverse_factor_rows([block[i : i + ROWS] for i in range(0, width, ROWS)], 4, 1)
        inverse = jnp.where(column <= row, jnp.concatenate(tiles, axis=0), 0.0)
        if end < n:
            near = precise_dot(work[end : end + width, begin:end], inverse, ((1,), (1,)))
            diagonal = work[end : end + width, end : end + width] - precise_dot(near, near, ((1,), (1,)))
            far = precise_dot(work[end + width :, begin:end], inverse, ((1,), (1,)))
            below = jnp.concatenate([near, far], axis=0)
        else:
            below = precise_dot(work[end:, begin:end], inverse, ((1,), (1,)))
        if begin > 0:
            work[begin:end, :begin] = precise_dot(inverse, work[begin:end, :begin])
            work[end:, :begin] = work[end:, :begin] - precise_dot(below, work[begin:end, :begin])
        work[begin:end, begin:end] = inverse
        work[end:, begin:end] = -precise_dot(below, inverse)
        if end + width < n:
            work[end + width :, end : end + width] = work[end + width :, end : end + width] - precise_dot(far, near, ((1,), (1,)))
            work[end + width :, end + width :] = work[end + width :, end + width :] - precise_dot(
                far, far[: n - end - width], ((1,), (1,))
            )
        elif end < n:
            work[n:, end:] = work[n:, end:] - precise_dot(far, near, ((1,), (1,)))
    shift = -work[n : n + 1, :]
    copies = []
    for begin in range(0, n, width):
        rows = slice(begin, begin + width)
        place = lax.broadcasted_iota(jnp.int32, (width, n), 0) + begin
        lower = lax.broadcasted_iota(jnp.int32, (width, n), 1) <= place
        mixing = (jnp.where(lower, work[rows, :] * math.sqrt(n - 1.0), 0.0) + shift).astype(jnp.bfloat16)
        out[rows, :] = mean_ref[...] + jnp.dot(mixing, anomaly_ref[...], preferred_element_type=F32)
        copies.append(pltpu.make_async_copy(out.at[rows], out_hbm.at[rows], sems.at[begin // width]))
        copies[-1].start()
    for copy in copies:
        copy.wait()


def analysis(packed, pull_tile, anomaly, mean):
    n, here = anomaly.shape
    return pl.pallas_call(
        functools.partial(analysis_kernel, n, LANES),
        out_shape=jax.ShapeDtypeStruct((n, here), F32),
        in_specs=[pl.BlockSpec(memory_space=pltpu.VMEM)] * 4,
        out_specs=pl.BlockSpec(memory_space=pltpu.HBM),
        scratch_shapes=[
            pltpu.VMEM((n + ROWS, n), F32),
            pltpu.VMEM((n, here), F32),
            pltpu.SemaphoreType.DMA((n // LANES,)),
        ],
        compiler_params=pltpu.CompilerParams(vmem_limit_bytes=24 << 20),
        name="analysis",
    )(packed, pull_tile, anomaly, mean)


def local(
    background_copies,
    measuring_span_leading_cell,
    measuring_kernel_coefficients,
    measured_readings,
    measured_error_precision,
):
    total, pulled, copy_anomalies, predicted_centroid = front(
        background_copies,
        measuring_span_leading_cell[None, :],
        jnp.transpose(measuring_kernel_coefficients),
        measured_readings[None, :],
        measured_error_precision[None, :],
        N_Y,
        lax.axis_size("cells") // N_Y,
    )
    return analysis(total, pulled, copy_anomalies, predicted_centroid)


def solution(mesh):
    in_specs = (
        P("mem", "cells"),
        P(("cells", "mem")),
        P(("cells", "mem"), None),
        P(("cells", "mem")),
        P(("cells", "mem")),
    )
    out_specs = P(None, ("cells", "mem"))
    return jax.shard_map(local, mesh=mesh, in_specs=in_specs, out_specs=out_specs, check_vma=False)
```

```python
import functools
import math

import jax
import jax.numpy as jnp
from jax import lax
from jax.experimental import pallas as pl
from jax.experimental.pallas import tpu as pltpu
from jax.sharding import PartitionSpec as P

F32 = jnp.float32
N_Y = 4
N_CORE = 2
ROWS, LANES = 8, 128
MESH = pl.DeviceIdType.MESH


def front_kernel(n_mem, n_y, n_z, field_ref, start_hbm, weight_hbm, reading_hbm, precision_hbm,
                 total_ref, pulled_ref, anomaly_ref, mean_ref,
                 start_ref, weight_ref, reading_ref, precision_ref, state, spread_out, table, weighted, local_sums, core_in, plane_out, plane_in, z_in,
                 small_sem, own_sem, edge_send, edge_recv, x_send, x_recv,
                 core_sem, plane_sem, z_sem, gather_sem, pair_sem):
    cell, mem = lax.axis_index("cells"), lax.axis_index("mem")
    n_cells = n_y * n_z
    y, z = lax.rem(cell, n_y), cell // n_y
    n_x = n_mem // N_CORE
    x, core = mem // N_CORE, lax.rem(mem, N_CORE)
    members = field_ref.shape[0]
    n = members * n_mem
    here = anomaly_ref.shape[1]
    wide = state.shape[1]
    edge = wide - here
    last = n_mem - 1

    def mem_peer(step):
        return (cell, lax.rem(mem + step, n_mem))

    n_plane = n_x * n_y
    spot_here = x * n_y + y

    def plane_peer(step):
        spot = lax.rem(spot_here + step, n_plane)
        return (z * n_y + lax.rem(spot, n_y), (spot // n_y) * N_CORE + core)

    def core_peer(step):
        return (cell, x * N_CORE + lax.rem(core + step, N_CORE))

    def z_peer(step):
        return (lax.rem(z + step, n_z) * n_y + y, mem)

    def signal(peer):
        pl.semaphore_signal(barrier, inc=1, device_id=peer, device_id_type=MESH)

    small = [
        pltpu.make_async_copy(source, target, small_sem.at[index])
        for index, (source, target) in enumerate(
            ((start_hbm, start_ref), (weight_hbm, weight_ref), (reading_hbm, reading_ref), (precision_hbm, precision_ref))
        )
    ]
    for copy in small:
        copy.start()

    barrier = pltpu.get_barrier_semaphore()
    for step in range(1, n_mem):
        signal(mem_peer(step))
    for step in range(1, n_plane):
        signal(plane_peer(step))
    for step in range(1, n_z):
        signal(z_peer(step))

    @pl.when(mem == last)
    def _():
        for source in range(n_mem):
            signal((lax.rem(cell + 1, n_cells), source))

    rows_here = pl.ds(pl.multiple_of(mem * members, members), members)

    def own_copy(width):
        return pltpu.make_async_copy(
            field_ref.at[:, pl.ds(pl.multiple_of(mem * here, here), width)],
            state.at[rows_here, pl.ds(0, width)], own_sem,
        )

    @pl.when(mem != last)
    def _():
        own_copy(wide).start()

    @pl.when(mem == last)
    def _():
        own_copy(here).start()

    pl.semaphore_wait(barrier, n_mem + n_plane + n_z - 2)

    def slab_copy(step, width):
        target = lax.rem(mem + step, n_mem)
        return pltpu.make_async_remote_copy(
            src_ref=field_ref.at[:, pl.ds(pl.multiple_of(target * here, here), width)],
            dst_ref=state.at[rows_here, pl.ds(0, width)],
            send_sem=x_send.at[step - 1], recv_sem=x_recv.at[step - 1],
            device_id=mem_peer(step), device_id_type=MESH,
        )

    def arrival(step, width):
        source = lax.rem(mem + n_mem - step, n_mem)
        rows = pl.ds(pl.multiple_of(source * members, members), members)
        return pltpu.make_async_remote_copy(
            src_ref=field_ref.at[:, pl.ds(0, width)], dst_ref=state.at[rows, pl.ds(0, width)],
            send_sem=x_send.at[step - 1], recv_sem=x_recv.at[step - 1],
            device_id=mem_peer(step), device_id_type=MESH,
        )

    def edge_copy(source):
        rows = pl.ds(pl.multiple_of(source * members, members), members)
        return pltpu.make_async_remote_copy(
            src_ref=field_ref.at[:, pl.ds(0, edge)], dst_ref=state.at[rows, pl.ds(here, edge)],
            send_sem=edge_send, recv_sem=edge_recv.at[source],
            device_id=(lax.rem(cell + n_cells - 1, n_cells), last), device_id_type=MESH,
        )

    for step in range(1, n_mem):
        target = lax.rem(mem + step, n_mem)

        @pl.when(target != last)
        def _(step=step):
            slab_copy(step, wide).start()

        @pl.when(target == last)
        def _(step=step):
            slab_copy(step, here).start()

    edge_copy(mem).start()

    for copy in small:
        copy.wait()
    start = start_ref[...]
    taps = [weight_ref[j : j + 1, :].astype(F32) for j in range(weight_ref.shape[0])]
    chunk = 64

    @pl.loop(0, wide // chunk)
    def _(index):
        first = pl.multiple_of(index * chunk, chunk)
        ahead = lax.broadcasted_iota(jnp.int32, (chunk, start.shape[1]), 0) + first - start
        block = jnp.zeros(ahead.shape, F32)
        for j, tap in enumerate(taps):
            block = jnp.where(ahead == j, tap, block)
        table[pl.ds(first, chunk), :] = block.astype(jnp.bfloat16)

    step_rows = 64

    def row_sums(source):
        rows = pl.ds(pl.multiple_of(source * members, members), members)
        return jnp.sum(state[rows, :].astype(F32).reshape(members // ROWS, ROWS, wide), axis=0)

    @pl.when(mem != last)
    def _():
        own_copy(wide).wait()

    @pl.when(mem == last)
    def _():
        own_copy(here).wait()
        edge_copy(mem).wait_recv()

    sums = row_sums(mem)
    for step in range(1, n_mem):
        source = lax.rem(mem + n_mem - step, n_mem)

        @pl.when(mem != last)
        def _(step=step):
            arrival(step, wide).wait_recv()

        @pl.when(mem == last)
        def _(step=step, source=source):
            arrival(step, here).wait_recv()
            edge_copy(source).wait_recv()

        sums = sums + row_sums(source)
    mean = jnp.sum(sums, axis=0, keepdims=True) / n
    mean_ref[...] = mean[:, :here]

    @pl.loop(0, n // step_rows)
    def _(index):
        rows = pl.ds(pl.multiple_of(index * step_rows, step_rows), step_rows)
        away = (state[rows, :].astype(F32) - mean).astype(jnp.bfloat16)
        spread_out[rows, :] = away
        anomaly_ref[rows, :] = away[:, :here]

    high = mean.astype(jnp.bfloat16)
    rest = mean - high.astype(F32)
    middle = rest.astype(jnp.bfloat16)
    small = (rest - middle.astype(F32)).astype(jnp.bfloat16)
    spread_out[n:, :] = jnp.concatenate([high, middle, small, jnp.zeros((13, wide), jnp.bfloat16)], axis=0)
    projected = jnp.dot(spread_out[...], table[...], preferred_element_type=F32)
    root = jnp.sqrt(precision_ref[...])
    observed = projected[n : n + 1] + (projected[n + 1 : n + 2] + projected[n + 2 : n + 3])
    innovation = (root * (reading_ref[...] - observed)).astype(jnp.bfloat16)
    weighted[:n, :] = (root * projected[:n]).astype(jnp.bfloat16)
    weighted[n:, :] = jnp.concatenate([innovation, jnp.zeros((15, innovation.shape[1]), jnp.bfloat16)], axis=0)

    part = plane_out.shape[1] - ROWS
    half = n_plane * part
    place = 0
    pull = []
    for begin in range(0, n, LANES):
        product = lax.dot_general(
            weighted[begin:, :], weighted[begin : begin + LANES, :], (((1,), (1,)), ((), ())), preferred_element_type=F32
        )
        pull.append(product[n - begin : n - begin + 1])
        for row in range(0, n - begin, ROWS):
            side, spot = place // half, place % half
            local_sums[side, spot // part, spot % part : spot % part + ROWS, :] = product[row : row + ROWS]
            place += ROWS
    pull_tile = jnp.concatenate(pull + [jnp.zeros((ROWS - len(pull), LANES), F32)], axis=0)
    for side in range(N_CORE):
        for s in range(n_plane):
            local_sums[side, s, part:, :] = pull_tile

    def begin_all(sources, target, peer, sems, count):
        copies = [
            pltpu.make_async_remote_copy(
                src_ref=sources(step), dst_ref=target(step), send_sem=sems.at[0, step - 1], recv_sem=sems.at[1, step - 1],
                device_id=peer(step), device_id_type=MESH,
            )
            for step in range(1, count)
        ]
        for copy in copies:
            copy.start()
        pending.extend(copies)
        return copies

    def arrived(copies):
        for copy in copies:
            copy.wait_recv()

    pending = []
    other = lax.rem(core + 1, N_CORE)
    arrived(begin_all(lambda s: local_sums.at[other], lambda s: core_in, core_peer, core_sem, N_CORE))
    plane_out[...] = local_sums[core] + core_in[...]
    shares = begin_all(
        lambda s: plane_out.at[lax.rem(spot_here + s, n_plane)], lambda s: plane_in.at[s - 1], plane_peer, plane_sem, n_plane
    )
    summed = plane_out[spot_here]
    for s, share in enumerate(shares):
        share.wait_recv()
        summed = summed + plane_in[s]
    z_in[z] = summed
    arrived(begin_all(lambda s: z_in.at[z], lambda s: z_in.at[z], z_peer, z_sem, n_z))
    summed = z_in[0]
    for s in range(1, n_z):
        summed = summed + z_in[s]
    pulled_ref[...] = summed[part:]
    base = core * half
    own = pl.ds(pl.multiple_of(base + spot_here * part, ROWS), part)
    total_ref[own, :] = summed[:part]
    arrived(begin_all(lambda s: total_ref.at[own], lambda s: total_ref.at[own], plane_peer, gather_sem, n_plane))
    mine = pl.ds(pl.multiple_of(base, ROWS), half)
    arrived(begin_all(lambda s: total_ref.at[mine], lambda s: total_ref.at[mine], core_peer, pair_sem, N_CORE))
    for copy in pending:
        copy.wait_send()
    edge_copy(mem).wait_send()
    for step in range(1, n_mem):
        target = lax.rem(mem + step, n_mem)

        @pl.when(target != last)
        def _(step=step):
            slab_copy(step, wide).wait_send()

        @pl.when(target == last)
        def _(step=step):
            slab_copy(step, here).wait_send()


def front(field, start, weights, readings, precision, n_y, n_z):
    members, slab = field.shape
    n_mem = lax.axis_size("mem")
    n, here = members * n_mem, slab // n_mem
    observations = start.shape[1]
    blocks = n // LANES
    packed = LANES * blocks * (blocks + 1) // 2
    n_plane = n_mem // N_CORE * n_y
    part = packed // (N_CORE * n_plane)
    dma = pltpu.SemaphoreType.DMA
    vmem = pl.BlockSpec(memory_space=pltpu.VMEM)
    bf16 = jnp.bfloat16
    return pl.pallas_call(
        functools.partial(front_kernel, n_mem, n_y, n_z),
        out_shape=(
            jax.ShapeDtypeStruct((packed, LANES), F32),
            jax.ShapeDtypeStruct((ROWS, LANES), F32),
            jax.ShapeDtypeStruct((n, here), bf16),
            jax.ShapeDtypeStruct((1, here), F32),
        ),
        in_specs=[pl.BlockSpec(memory_space=pltpu.HBM)] * 5,
        out_specs=(vmem,) * 4,
        scratch_shapes=[
            pltpu.VMEM(start.shape, start.dtype),
            pltpu.VMEM(weights.shape, weights.dtype),
            pltpu.VMEM(readings.shape, readings.dtype),
            pltpu.VMEM(precision.shape, precision.dtype),
            pltpu.VMEM((n, here + LANES), bf16),
            pltpu.VMEM((n + 16, here + LANES), bf16),
            pltpu.VMEM((here + LANES, observations), bf16),
            pltpu.VMEM((n + 16, observations), bf16),
            pltpu.VMEM((N_CORE, n_plane, part + ROWS, LANES), F32),
            pltpu.VMEM((n_plane, part + ROWS, LANES), F32),
            pltpu.VMEM((n_plane, part + ROWS, LANES), F32),
            pltpu.VMEM((n_plane - 1, part + ROWS, LANES), F32),
            pltpu.VMEM((n_z, part + ROWS, LANES), F32),
            dma((4,)), dma, dma, dma((n_mem,)), dma((n_mem - 1,)), dma((n_mem - 1,)),
            dma((2, N_CORE - 1)), dma((2, n_plane - 1)), dma((2, n_z - 1)), dma((2, n_plane - 1)), dma((2, N_CORE - 1)),
        ],
        compiler_params=pltpu.CompilerParams(collective_id=0, has_side_effects=True, vmem_limit_bytes=20 << 20),
        name="front",
    )(*(pltpu.with_memory_space_constraint(x, pltpu.HBM) for x in (field, start, weights, readings, precision)))

def precise_dot(left, right, contract=((1,), (0,))):
    return lax.dot_general(
        left, right, (contract, ((), ())), precision=lax.Precision.HIGHEST, preferred_element_type=F32
    )


def inverse_factor_rows(tiles, panel, ahead):
    tiles = list(tiles)
    count = len(tiles)
    extent = tiles[0].shape[1]
    lane = lax.broadcasted_iota(jnp.int32, (ROWS, extent), 1)
    sublane = lax.broadcasted_iota(jnp.int32, (ROWS, extent), 0)

    def spread(value):
        return jnp.broadcast_to(value, (ROWS, extent))

    def pick(tile, position):
        return jnp.take_along_axis(tile, jnp.full((ROWS, extent), position, jnp.int32), axis=1)

    for home in range(count):
        first = home * ROWS
        panel_end = min((home // panel + 1) * panel, count)
        near_end = max(min(panel_end + ahead, count), min(home + 2, count))
        own = tiles[home]
        lanes = later if home else [pick(own, first + a) for a in range(ROWS)]
        pivots = {(b, a): spread(lanes[a][b : b + 1, :]) for a in range(ROWS) for b in range(a, ROWS)}
        member = (lane >= first) & (lane < first + ROWS)
        rows = [
            jnp.where(member, jnp.where(lane == first + a, 1.0, 0.0), spread(own[a : a + 1, :])) for a in range(ROWS)
        ]
        scales = []
        following = tiles[home + 1] if home + 1 < count else None
        if following is not None:
            columns = [pick(following, first + a) for a in range(ROWS)]
            later = [pick(following, first + ROWS + c) for c in range(ROWS)]
            following = jnp.where(member, 0.0, following)
        for a in range(ROWS):
            scale = lax.rsqrt(pivots[(a, a)])
            scales.append(scale)
            rows[a] = rows[a] * scale
            for b in range(a + 1, ROWS):
                pivots[(b, a)] = pivots[(b, a)] * scale
            for b in range(a + 1, ROWS):
                for c in range(a + 1, b + 1):
                    pivots[(b, c)] = pivots[(b, c)] - pivots[(b, a)] * pivots[(c, a)]
                rows[b] = rows[b] - pivots[(b, a)] * rows[a]
            if following is not None:
                columns[a] = columns[a] * scale
                for b in range(a + 1, ROWS):
                    columns[b] = columns[b] - columns[a] * pivots[(b, a)]
                following = following - columns[a] * rows[a]
                later = [part - columns[a] * spread(columns[a][c : c + 1, :]) for c, part in enumerate(later)]
        fresh = rows[0]
        for a in range(1, ROWS):
            fresh = jnp.where(sublane == a, rows[a], fresh)
        tiles[home] = fresh
        solved = list(rows)
        for a in range(ROWS - 1, -1, -1):
            solved[a] = solved[a] * scales[a]
            for b in range(a):
                solved[b] = solved[b] - pivots[(a, b)] * solved[a]
        if following is not None:
            tiles[home + 1] = following
        for index in range(home + 2, near_end):
            tile = tiles[index]
            fresh = jnp.where(member, 0.0, tile)
            for a in range(ROWS):
                fresh = fresh - pick(tile, first + a) * solved[a]
            tiles[index] = fresh
        if home + 1 == panel_end and near_end < count:
            begin = (home // panel) * panel
            done = tiles[begin:panel_end]
            masked = [
                jnp.where((lane >= (begin + i + 1) * ROWS) & (lane < panel_end * ROWS), 0.0, tile)
                for i, tile in enumerate(done)
            ]
            change = precise_dot(jnp.concatenate(done, axis=0), jnp.concatenate(masked, axis=0), ((0,), (0,)))
            inside = (lane >= begin * ROWS) & (lane < panel_end * ROWS)
            for index in range(near_end, count):
                tiles[index] = jnp.where(inside, 0.0, tiles[index]) - change[index * ROWS : (index + 1) * ROWS]
    return tiles


def analysis_kernel(n, width, packed_ref, pull_ref, anomaly_ref, mean_ref, out_hbm, work, out, sems):
    shape = (width, width)
    row = lax.broadcasted_iota(jnp.int32, shape, 0)
    column = lax.broadcasted_iota(jnp.int32, shape, 1)
    unit = jnp.where(row == column, 1.0, 0.0)
    place = 0
    for begin in range(0, n, width):
        work[begin:n, begin : begin + width] = packed_ref[place : place + n - begin, :]
        place += n - begin
        index = begin // width
        work[n : n + 1, begin : begin + width] = pull_ref[index : index + 1, :]
    work[n + 1 :, :] = jnp.zeros((ROWS - 1, n), F32)
    diagonal = work[:width, :width]
    for begin in range(0, n, width):
        end = begin + width
        block = diagonal + (n - 1.0) * unit
        tiles = inverse_factor_rows([block[i : i + ROWS] for i in range(0, width, ROWS)], 4, 1)
        inverse = jnp.where(column <= row, jnp.concatenate(tiles, axis=0), 0.0)
        if end < n:
            near = precise_dot(work[end : end + width, begin:end], inverse, ((1,), (1,)))
            diagonal = work[end : end + width, end : end + width] - precise_dot(near, near, ((1,), (1,)))
            far = precise_dot(work[end + width :, begin:end], inverse, ((1,), (1,)))
            below = jnp.concatenate([near, far], axis=0)
        else:
            below = precise_dot(work[end:, begin:end], inverse, ((1,), (1,)))
        if begin > 0:
            work[begin:end, :begin] = precise_dot(inverse, work[begin:end, :begin])
            work[end:, :begin] = work[end:, :begin] - precise_dot(below, work[begin:end, :begin])
        work[begin:end, begin:end] = inverse
        work[end:, begin:end] = -precise_dot(below, inverse)
        if end + width < n:
            work[end + width :, end : end + width] = work[end + width :, end : end + width] - precise_dot(far, near, ((1,), (1,)))
            work[end + width :, end + width :] = work[end + width :, end + width :] - precise_dot(
                far, far[: n - end - width], ((1,), (1,))
            )
        elif end < n:
            work[n:, end:] = work[n:, end:] - precise_dot(far, near, ((1,), (1,)))
    shift = -work[n : n + 1, :]
    copies = []
    for begin in range(0, n, width):
        rows = slice(begin, begin + width)
        place = lax.broadcasted_iota(jnp.int32, (width, n), 0) + begin
        lower = lax.broadcasted_iota(jnp.int32, (width, n), 1) <= place
        mixing = (jnp.where(lower, work[rows, :] * math.sqrt(n - 1.0), 0.0) + shift).astype(jnp.bfloat16)
        out[rows, :] = mean_ref[...] + jnp.dot(mixing, anomaly_ref[...], preferred_element_type=F32)
        copies.append(pltpu.make_async_copy(out.at[rows], out_hbm.at[rows], sems.at[begin // width]))
        copies[-1].start()
    for copy in copies:
        copy.wait()


def analysis(packed, pull_tile, anomaly, mean):
    n, here = anomaly.shape
    return pl.pallas_call(
        functools.partial(analysis_kernel, n, LANES),
        out_shape=jax.ShapeDtypeStruct((n, here), F32),
        in_specs=[pl.BlockSpec(memory_space=pltpu.VMEM)] * 4,
        out_specs=pl.BlockSpec(memory_space=pltpu.HBM),
        scratch_shapes=[
            pltpu.VMEM((n + ROWS, n), F32),
            pltpu.VMEM((n, here), F32),
            pltpu.SemaphoreType.DMA((n // LANES,)),
        ],
        compiler_params=pltpu.CompilerParams(vmem_limit_bytes=24 << 20),
        name="analysis",
    )(packed, pull_tile, anomaly, mean)


def local(
    background_copies,
    measuring_span_leading_cell,
    measuring_kernel_coefficients,
    measured_readings,
    measured_error_precision,
):
    total, pulled, copy_anomalies, predicted_centroid = front(
        background_copies,
        measuring_span_leading_cell[None, :],
        jnp.transpose(measuring_kernel_coefficients),
        measured_readings[None, :],
        measured_error_precision[None, :],
        N_Y,
        lax.axis_size("cells") // N_Y,
    )
    return analysis(total, pulled, copy_anomalies, predicted_centroid)


def solution(mesh):
    in_specs = (
        P("mem", "cells"),
        P(("cells", "mem")),
        P(("cells", "mem"), None),
        P(("cells", "mem")),
        P(("cells", "mem")),
    )
    out_specs = P(None, ("cells", "mem"))
    return jax.shard_map(local, mesh=mesh, in_specs=in_specs, out_specs=out_specs, check_vma=False)
```
